256 devices in a mesh: expert: 32 (over y, z), vocab: 8 (over x, core).
Axes of the slice: x: 4, y: 4, z: 8, core: 2. Of those that a mesh axis runs over, the one named last changes fastest.
Arguments:
- layer_out: bfloat16 [1024, 2048], P('expert'), may hold values from -6 to 6
- moe_input: bfloat16 [1024, 2048], P('expert'), may hold values from -6 to 6
- final_gain: float32 [2048], replicated, may hold values from 0.1 to 1.9
- head_weight: bfloat16 [2048, 98304], P(None, ('expert', 'vocab')), may hold values from -0.125 to 0.125
- clean_ids: int32 [1024], P('expert'), may hold values from 0 to 98303
- levels: int32 [1024], P('expert'), may hold values from 0 to 15
- ratio_table: float32 [16], replicated, may hold values from 0.5 to 8
- gate_weights: float32 [1024, 8], P('expert'), may hold values from 0.05 to 0.5
- expert_ids: int32 [1024, 8], P('expert'), may hold values from 0 to 63, all different within a row; in each aligned block of 32 rows (0 to 31, 32 to 63, ...) at most 8 rows name the same one
- w_gate: bfloat16 [64, 2048, 1024], P('expert', None, 'vocab'), may hold values from -0.125 to 0.125
- w_up: bfloat16 [64, 2048, 1024], P('expert', None, 'vocab'), may hold values from -0.125 to 0.125
- w_down: bfloat16 [64, 1024, 2048], P('expert', 'vocab'), may hold values from -0.1875 to 0.1875
Outputs:
- head_grad: float32 [2048, 98304], P(None, ('expert', 'vocab'))
- residual_grad: float32 [1024, 2048], P('expert', 'vocab')
- input_grad: float32 [1024, 2048], P('expert', 'vocab')
The draws below stay inside these ranges and needn't reach their ends.
Inputs may be any that keep to these rules, and one draw needn't show every extreme that they name: `expert_ids`: the 8 experts of a row are distinct; among the 32 rows of one index of expert no expert is named by more than 8 rows.
All inputs are finite; a program needn't handle non-finite values.
Results may differ from the reference program's by a relative error of at most 0.0044.
The reference program's roundings to bfloat16 on the way (of `normed`, `score_grad` and `routed_grad`) count: a program that leaves them out, or rounds other values in their place, can miss the bound.
Values may be sent and summed in bfloat16 or wider, within the bound.
No kernel may reach another device: no remote copies, remote signals or barrier semaphores. Data moves between devices by JAX's collectives and lax.ppermute only.
A program may use at most 64 MiB of HBM per device.

```python
import math
import jax
import jax.numpy as jnp
import numpy as np
from jax import lax

D = 2048
FF = 1024
TOP = 8
VOC_DEV = 384
ROWS_DEV = 32
LEVELS = 16
EXPERTS = 64
VOCAB = 98304
ROWS = 1024
CAP = 8
N_EXPERT = 32
N_VOCAB = 8


def touch_ends(values, key, low, top_value):
    spot = [jax.random.randint(jax.random.fold_in(key, axis), (), 0, length) for axis, length in enumerate(values.shape)]
    widest = values.shape.index(max(values.shape))
    next_to = spot[:widest] + [(spot[widest] + 1) % values.shape[widest]] + spot[widest + 1:]
    return values.at[tuple(spot)].set(low).at[tuple(next_to)].set(top_value)


def level_of(rng, shape, shards, smallest, top_value):
    gain, own = 1.0, jax.random.fold_in(rng, 6)
    for dim, parts in shards:
        draws = jnp.exp(jax.random.uniform(jax.random.fold_in(own, dim), (parts,), jnp.float32, smallest / len(shards), top_value / len(shards)))
        gain = gain * jnp.repeat(draws, shape[dim] // parts).reshape([-1 if axis == dim else 1 for axis in range(len(shape))])
    return gain


def skewed_wide(key, extent, number_of, skew):
    weights = [min(1 << octave, number_of + 1 - (1 << octave)) * (1 << 20) // math.isqrt((1 << octave) ** skew) + 1 for octave in range((number_of + 1).bit_length()) if 1 << octave <= number_of]
    width = 1 + sum(weights) // (1 << 30)
    listing = np.cumsum(np.array([max(1, weight // width) for weight in weights]))
    ticket = jax.random.randint(jax.random.fold_in(key, 1), extent, 0, int(listing[len(weights) - 1]))
    start = jnp.left_shift(1, jnp.searchsorted(jnp.asarray(listing, jnp.int32), ticket, side="right").astype(jnp.int32))
    grade = start - 1 + jax.random.randint(jax.random.fold_in(key, 4), extent, 0, 1 << 30) % jnp.minimum(start, number_of + 1 - start)
    return jax.random.permutation(jax.random.fold_in(key, 2), number_of)[grade].astype(jnp.int32)


def deal_out(key, own, number, rows, amount, top, most, slope):
    sequence = jax.random.permutation(key, amount)
    packed, usual = shares(amount, rows * top, most, slope, True), shares(amount, rows * top, most, slope, False)
    places = jnp.arange(amount)

    def named(sizes, rotation):
        used = int((sizes > 0).sum())
        fixed = max(1, used // 4)
        shifted = fixed + (places - fixed + rotation * (used - fixed)) % max(1, amount - fixed)
        return jnp.zeros((amount,), jnp.int32).at[sequence[jnp.where(places < fixed, places, shifted)]].set(jnp.asarray(sizes, jnp.int32))

    sizes = jnp.where(number % 4 == 0, named(packed, number // 4), named(usual, number - number // 4 - 1))
    mixed = jax.random.permutation(jax.random.fold_in(own, 3), amount)
    source_of, sink = mixed[0:amount // 2 * 2:2], mixed[1:amount // 2 * 2:2]
    margin = jnp.minimum(sizes[source_of] - 1, most - sizes[sink]) // 2
    margin = jnp.where((source_of == sequence[0]) | (sink == sequence[0]) | (sizes[sink] == 0), 0, jnp.maximum(margin, 0))
    shifted = jax.random.randint(jax.random.fold_in(own, 4), (amount // 2,), 0, 1 << 20) % (margin + 1)
    sizes = sizes.at[source_of].add(-shifted).at[sink].add(shifted)
    items = jnp.searchsorted(jnp.cumsum(sizes), jnp.arange(rows * top), side="right").astype(jnp.int32)
    table = items.reshape(top, rows).T
    table = table[jax.random.permutation(jax.random.fold_in(own, 1), rows)]
    rotation = jax.random.randint(jax.random.fold_in(own, 2), (rows, 1), 0, top)
    return jnp.take_along_axis(table, (jnp.arange(top)[None, :] + rotation) % top, axis=1)


def shares(number_of, total, bound, slope, full):
    loads = [(1 << 20) // math.isqrt(rank ** slope) + 1 for rank in range(1, number_of + 1)]
    largest = bound if full else min(bound, max(-(-total // number_of), total * loads[0] // sum(loads)))
    least = 1 if total - largest >= number_of - 1 else 0
    counts, spare = [largest] + [least] * (number_of - 1), total - largest - least * (number_of - 1)
    while spare > 0:
        candidates = [i for i in range(1, number_of) if counts[i] < largest] or [i for i in range(1, number_of) if counts[i] < bound]
        pool, budget = sum([loads[i] for i in candidates]), spare
        for i in candidates:
            extra = min(bound - counts[i], max(1, budget * loads[i] // pool), spare)
            counts[i] = counts[i] + extra
            spare = spare - extra
    return np.array(counts)


def scatter_about(own_key, dims, width, reach, cuts=(), kind=jnp.bfloat16):
    result = jax.random.normal(own_key, dims, jnp.float32) * width
    if len(cuts) > 0:
        result = level_of(own_key, dims, cuts, -0.22, 0.18) * result
    return jnp.clip(result, min=-reach, max=reach).astype(kind)


def setup_inputs(seed: int = 0) -> dict:
    streams_of = jax.random.split(jax.random.key(seed), 13)
    layer_out = scatter_about(streams_of[0], (ROWS, D), 1.0, 6.0, ((0, 32),))
    moe_input = scatter_about(streams_of[1], (ROWS, D), 1.0, 6.0, ((0, 32),))
    final_gain = jnp.clip(1.0 + 0.18 * jax.random.normal(streams_of[2], (D,), jnp.float32), 0.1, 1.9)
    head_weight = scatter_about(streams_of[3], (D, VOCAB), D ** -0.5, 0.125, ((1, 256),))
    clean_ids = touch_ends(skewed_wide(streams_of[4], (ROWS,), VOCAB, 2), jax.random.fold_in(streams_of[4], 3), 0, VOCAB - 1).astype(jnp.int32)
    levels = touch_ends(jax.random.randint(streams_of[5], (ROWS,), 0, LEVELS), jax.random.fold_in(streams_of[5], 1), 0, LEVELS - 1).astype(jnp.int32)
    ratio_table = jnp.clip(jnp.exp(jax.random.uniform(streams_of[6], (LEVELS,), jnp.float32, math.log(0.5), math.log(8.0))), 0.5, 8.0)
    gate_weights = jnp.clip(jnp.exp(math.log(0.5) - 2.3025851 * jax.random.uniform(streams_of[7], (ROWS, TOP), jnp.float32) ** level_of(streams_of[7], (ROWS, TOP), ((0, 32),), -0.2, 0.2)), 0.05, 0.5)
    expert_ids_keys = jax.random.split(jax.random.fold_in(streams_of[8], 1), ROWS // ROWS_DEV)
    expert_ids_turns = jax.random.permutation(jax.random.fold_in(streams_of[8], 3), ROWS // ROWS_DEV)
    expert_ids = jax.vmap(lambda own, number: deal_out(jax.random.fold_in(streams_of[8], 2), own, number, ROWS_DEV, EXPERTS, TOP, CAP, 2))(expert_ids_keys, expert_ids_turns).reshape((ROWS, TOP))
    w_gate = scatter_about(streams_of[9], (EXPERTS, D, FF), D ** -0.5, 0.125, ((0, 32), (2, 8)))
    w_up = scatter_about(streams_of[10], (EXPERTS, D, FF), D ** -0.5, 0.125, ((0, 32), (2, 8)))
    w_down = scatter_about(streams_of[11], (EXPERTS, FF, D), FF ** -0.5, 0.1875, ((0, 32), (1, 8)))
    return {"layer_out": layer_out, "moe_input": moe_input, "final_gain": final_gain, "head_weight": head_weight, "clean_ids": clean_ids, "levels": levels, "ratio_table": ratio_table, "gate_weights": gate_weights, "expert_ids": expert_ids, "w_gate": w_gate, "w_up": w_up, "w_down": w_down}


epsilon = 1e-05

def slot_positions(expert_ids):
    id_blocks = expert_ids.reshape(N_EXPERT, ROWS_DEV * TOP)
    labels = jnp.arange(EXPERTS, dtype=jnp.int32)
    onehot = (id_blocks[:, :, None] == labels[None, None, :]).astype(jnp.int32)
    earlier = jnp.cumsum(onehot, axis=1) - onehot
    slot_index = lax.optimization_barrier(jnp.sum(earlier * onehot, axis=2))
    source = jnp.arange(N_EXPERT, dtype=jnp.int32)[:, None]
    position = id_blocks * (N_EXPERT * CAP) + source * CAP + slot_index
    return position.reshape(-1).astype(jnp.int32)

def expert_backward(operands):
    inputs_slot, grads_slot, gate_matrix, up_matrix, down_matrix = operands
    inputs_wide = inputs_slot.astype(jnp.float32)
    gate_pre = jnp.dot(inputs_wide, gate_matrix.astype(jnp.float32), preferred_element_type=jnp.float32)
    up_pre = jnp.dot(inputs_wide, up_matrix.astype(jnp.float32), preferred_element_type=jnp.float32)
    act_grad = jnp.dot(grads_slot.astype(jnp.float32), down_matrix.astype(jnp.float32).T, preferred_element_type=jnp.float32)
    sigmoid_gate = jax.nn.sigmoid(gate_pre)
    gate_grad = (act_grad * up_pre * sigmoid_gate * (1.0 + gate_pre * (1.0 - sigmoid_gate))).astype(jnp.bfloat16)
    up_grad = (act_grad * gate_pre * sigmoid_gate).astype(jnp.bfloat16)
    first = jnp.dot(gate_grad.astype(jnp.float32), gate_matrix.astype(jnp.float32).T, preferred_element_type=jnp.float32)
    second = jnp.dot(up_grad.astype(jnp.float32), up_matrix.astype(jnp.float32).T, preferred_element_type=jnp.float32)
    return first + second

def reference(layer_out, moe_input, final_gain, head_weight, clean_ids, levels, ratio_table, gate_weights, expert_ids, w_gate, w_up, w_down):
    values = layer_out.astype(jnp.float32)
    row_scale = jnp.sqrt(lax.optimization_barrier(jnp.mean(values * values, axis=1, keepdims=True)) + epsilon)
    unit_rows = values / row_scale
    normed = (unit_rows * final_gain[None, :]).astype(jnp.bfloat16)
    normed_wide = normed.astype(jnp.float32)
    ratio_rows = ratio_table[levels]
    loss_scale = 1.0 / math.sqrt(ROWS)
    block_count = N_EXPERT * N_VOCAB
    weight_blocks = head_weight.reshape(D, block_count, VOC_DEV).transpose(1, 0, 2)

    def scan_step(accumulated, block_input):
        weight_block, block_index = block_input
        weight_wide = weight_block.astype(jnp.float32)
        scores = jnp.dot(normed_wide, weight_wide, preferred_element_type=jnp.float32)
        columns = block_index * VOC_DEV + jnp.arange(VOC_DEV, dtype=jnp.int32)
        target_hit = (clean_ids[:, None] == columns[None, :]).astype(jnp.float32)
        score_grad = ((jnp.exp(scores) - ratio_rows[:, None] * target_hit) * loss_scale).astype(jnp.bfloat16)
        grad_wide = score_grad.astype(jnp.float32)
        block_grad = jnp.dot(normed_wide.T, grad_wide, preferred_element_type=jnp.float32)
        accumulated = accumulated + jnp.dot(grad_wide, weight_wide.T, preferred_element_type=jnp.float32)
        return (accumulated, block_grad)
    normed_grad, grad_blocks = lax.scan(scan_step, jnp.zeros((ROWS, D), jnp.float32), (weight_blocks, jnp.arange(block_count, dtype=jnp.int32)))
    head_grad = grad_blocks.transpose(1, 0, 2).reshape(D, VOCAB)
    gained = final_gain[None, :] * normed_grad
    residual_grad = (gained - unit_rows * lax.optimization_barrier(jnp.mean(unit_rows * gained, axis=1, keepdims=True))) / row_scale
    routed_grad = (gate_weights[:, :, None] * residual_grad[:, None, :]).astype(jnp.bfloat16).reshape(ROWS * TOP, D)
    inputs_rep = jnp.repeat(moe_input, TOP, axis=0)
    position = slot_positions(expert_ids)
    buffer_rows = EXPERTS * N_EXPERT * CAP
    inputs_buffer = jnp.zeros((buffer_rows, D), jnp.bfloat16).at[position].set(inputs_rep)
    grads_buffer = jnp.zeros((buffer_rows, D), jnp.bfloat16).at[position].set(routed_grad)
    slot_grads = lax.map(expert_backward, (inputs_buffer.reshape(EXPERTS, N_EXPERT * CAP, D), grads_buffer.reshape(EXPERTS, N_EXPERT * CAP, D), w_gate, w_up, w_down))
    per_pair = slot_grads.reshape(buffer_rows, D)[position]
    input_grad = lax.optimization_barrier(jnp.sum(per_pair.reshape(ROWS, TOP, D), axis=1))
    return (head_grad, residual_grad, input_grad)
```

```python
import math

import jax
import jax.numpy as jnp
from jax import lax
from jax.sharding import PartitionSpec as P

epsilon = 1e-05
YN, ZN, XN, CN = 4, 8, 4, 2
bf16 = jnp.bfloat16
f32 = jnp.float32


def wide_dot(a, b, dims, precision=None):
    return lax.dot_general(
        a, b, (dims, ((), ())), preferred_element_type=f32, precision=precision
    )


def along_y(a, step):
    moves = [
        (y * ZN + z, (y + step) % YN * ZN + z) for y in range(YN) for z in range(ZN)
    ]
    return lax.ppermute(a, "expert", moves)


def along_x(a, step):
    moves = [
        (x * CN + c, (x + step) % XN * CN + c) for x in range(XN) for c in range(CN)
    ]
    return lax.ppermute(a, "vocab", moves)


def across_core(a):
    moves = [(x * CN + c, x * CN + 1 - c) for x in range(XN) for c in range(CN)]
    return lax.ppermute(a, "vocab", moves)


def z_groups():
    return [[y * ZN + z for z in range(ZN)] for y in range(YN)]


def in_ring_order(a, move, ring):
    return [a] + [move(a, ring - k) for k in range(1, ring)]


def blocks_in_order(a, starts, width, axis):
    return jnp.concatenate(
        [lax.dynamic_slice_in_dim(a, s, width, axis) for s in starts], axis=axis
    )


def on_device(
    layer_out,
    moe_input,
    final_gain,
    head_weight,
    clean_ids,
    levels,
    ratio_table,
    gate_weights,
    expert_ids,
    w_gate,
    w_up,
    w_down,
):
    rows, width = layer_out.shape
    n_expert = lax.axis_size("expert")
    n_vocab = lax.axis_size("vocab")
    all_rows = rows * n_expert
    own_experts = w_gate.shape[0]
    experts = own_experts * n_expert
    capacity = max(2, 2 * rows * expert_ids.shape[1] // experts)
    share = width // n_vocab
    half = share // 2
    tile = head_weight.shape[1]
    e_at = lax.axis_index("expert")
    v_at = lax.axis_index("vocab")
    y_at = e_at // ZN
    x_at, c_at = v_at // CN, v_at % CN

    v_order = [
        ((x_at + k) % XN) * CN + (c_at + c) % CN for c in range(CN) for k in range(XN)
    ]
    head_order = [
        (((x_at + k) % XN) * CN + (c_at + c) % CN) * share + h * half
        for c in range(CN)
        for h in range(2)
        for k in range(XN)
    ]

    values = layer_out.astype(f32)
    row_scale = jnp.sqrt(jnp.mean(values * values, axis=1, keepdims=True) + epsilon)
    unit_share = (
        lax.dynamic_slice_in_dim(layer_out, v_at * share, share, 1).astype(f32) / row_scale
    )
    gain_share = lax.dynamic_slice_in_dim(final_gain, v_at * share, share, 0)[None, :]
    normed_share = (unit_share * gain_share).astype(bf16)

    moe_share = lax.dynamic_slice_in_dim(moe_input, v_at * share, share, 1)
    numbers = jnp.concatenate(
        [
            (clean_ids % 256)[:, None],
            (clean_ids // 256 % 256)[:, None],
            (clean_ids // 65536)[:, None],
            levels[:, None],
            expert_ids,
        ],
        axis=1,
    ).astype(bf16)
    numbers = jnp.pad(numbers, ((0, 0), (0, 128 - numbers.shape[1])))
    side_all = lax.all_gather(
        jnp.concatenate([moe_share, numbers], axis=1), "expert", axis=0, tiled=True
    )
    moe_all = side_all[:, :share]
    numbers_all = side_all[:, share:share + 16].astype(jnp.int32)

    along_z = lax.all_to_all(
        jnp.broadcast_to(normed_share[None], (ZN, rows, share)),
        "expert",
        0,
        0,
        axis_index_groups=z_groups(),
        tiled=True,
    ).reshape(ZN * rows, share)
    first = jnp.concatenate(in_ring_order(along_z[:, :half], along_y, YN), axis=0)
    second = jnp.concatenate(in_ring_order(along_z[:, half:], along_x, XN), axis=1)
    first = jnp.concatenate(in_ring_order(first, along_x, XN), axis=1)
    second = jnp.concatenate(in_ring_order(second, along_y, YN), axis=0)
    normed_all = jnp.concatenate(
        [first, second, across_core(first), across_core(second)], axis=1
    )

    head_turned = blocks_in_order(head_weight, head_order, half, 0)
    own_order = jnp.concatenate([numbers_all, numbers_all], axis=0)
    own_order = lax.dynamic_slice_in_dim(own_order, y_at * ZN * rows, all_rows, 0)
    clean_all = own_order[:, 0:1] + 256 * own_order[:, 1:2] + 65536 * own_order[:, 2:3]
    level_labels = jnp.arange(ratio_table.shape[0], dtype=jnp.int32)
    ratio_rows = jnp.sum(
        jnp.where(own_order[:, 3:4] == level_labels[None, :], ratio_table[None, :], 0.0),
        axis=1,
        keepdims=True,
    )
    columns = (e_at * n_vocab + v_at) * tile + jnp.arange(tile, dtype=jnp.int32)
    scores = wide_dot(normed_all, head_turned, ((1,), (0,)))
    target_hit = (clean_all == columns[None, :]).astype(f32)
    loss_scale = 1.0 / math.sqrt(all_rows)
    score_grad = lax.optimization_barrier(
        ((jnp.exp(scores) - ratio_rows * target_hit) * loss_scale).astype(bf16)
    )

    side = width // 2
    far = wide_dot(score_grad, head_turned[side:], ((1,), (1,))).astype(bf16)
    far = across_core(far)
    near = wide_dot(score_grad, head_turned[:side], ((1,), (1,)))
    near = near + far.astype(f32)

    quarter = all_rows // YN
    half_side = side // 2
    first = near[:, :half_side]
    second = near[:, half_side:]
    first_sent = [
        along_x(first[:, k * half:(k + 1) * half].astype(bf16), k) for k in range(1, XN)
    ]
    second_sent = [
        along_y(second[i * quarter:(i + 1) * quarter].astype(bf16), i) for i in range(1, YN)
    ]
    first = first[:, :half] + sum(a.astype(f32) for a in first_sent)
    second = second[:quarter] + sum(a.astype(f32) for a in second_sent)
    first = first[:quarter] + sum(
        along_y(first[i * quarter:(i + 1) * quarter], i) for i in range(1, YN)
    )
    second = second[:, :half] + sum(
        along_x(second[:, k * half:(k + 1) * half], k) for k in range(1, XN)
    )
    both = jnp.concatenate([first, second], axis=1).reshape(ZN, rows, share)
    normed_grad = jnp.sum(
        lax.all_to_all(both, "expert", 0, 0, axis_index_groups=z_groups(), tiled=True), axis=0
    )

    gained = gain_share * normed_grad
    total = jnp.sum(unit_share * gained, axis=1)
    total = total + across_core(total)
    total = total + sum(along_x(total, k) for k in range(1, XN))
    residual_grad = (gained - unit_share * (total / width)[:, None]) / row_scale

    def named_by(ids, labels):
        return (ids[..., :, None] == labels).astype(f32).sum(axis=-2)

    labels = jnp.arange(experts, dtype=jnp.int32)
    naming = named_by(expert_ids, labels)
    before = (jnp.arange(rows)[:, None] > jnp.arange(rows)[None, :]).astype(f32)
    earlier = wide_dot(before, naming, ((1,), (0,)))
    gates = jnp.sum(
        jnp.where(expert_ids[:, :, None] == labels, gate_weights[:, :, None], 0.0), axis=1
    )
    slots = jnp.arange(capacity, dtype=f32)
    taken = (earlier.T[:, None, :] == slots[None, :, None]) & (naming.T[:, None, :] > 0)
    slot_gate = jnp.sum(jnp.where(taken, gates.T[:, None, :], 0.0), axis=2)
    pick = taken.astype(f32).reshape(experts * capacity, rows)
    slot_gate = slot_gate.reshape(experts * capacity, 1)

    routed = wide_dot(pick, residual_grad, ((1,), (0,)), lax.Precision.HIGHEST)
    routed = (slot_gate * routed).astype(bf16).reshape(n_expert, own_experts * capacity, share)
    routed = lax.all_to_all(routed, "expert", 0, 0, tiled=True)

    def by_expert(a):
        a = a.reshape(n_expert, own_experts, capacity, a.shape[-1])
        return a.transpose(1, 0, 2, 3).reshape(own_experts, n_expert * capacity, a.shape[-1])

    grads = jnp.concatenate(in_ring_order(by_expert(routed), along_x, XN), axis=2)
    grads = jnp.concatenate([grads, across_core(grads)], axis=2)

    ids_all = numbers_all[:, 4:4 + expert_ids.shape[1]].reshape(n_expert, rows, -1)
    own_labels = e_at * own_experts + jnp.arange(own_experts, dtype=jnp.int32)
    naming_all = named_by(ids_all, own_labels)
    earlier_all = jnp.einsum("ij,sje->sie", before, naming_all)
    taken_all = (
        earlier_all.transpose(2, 0, 1)[:, :, None, :] == slots[None, None, :, None]
    ) & (naming_all.transpose(2, 0, 1)[:, :, None, :] > 0)
    inputs = jnp.einsum(
        "esqr,srd->esqd",
        taken_all.astype(bf16),
        moe_all.reshape(n_expert, rows, share),
        preferred_element_type=f32,
    ).astype(bf16)
    inputs = inputs.reshape(own_experts, n_expert * capacity, share)
    inputs = lax.all_gather(inputs, "vocab", axis=2, tiled=True)

    gate_turned = blocks_in_order(w_gate, [v * share for v in v_order], share, 1)
    up_turned = blocks_in_order(w_up, [v * share for v in v_order], share, 1)
    down_turned = blocks_in_order(w_down, [v * share for v in v_order], share, 2)
    gate_pre = jnp.einsum("esd,edf->esf", inputs, w_gate, preferred_element_type=f32)
    up_pre = jnp.einsum("esd,edf->esf", inputs, w_up, preferred_element_type=f32)
    act_grad = jnp.einsum("esd,efd->esf", grads, down_turned, preferred_element_type=f32)
    sigmoid_gate = jax.nn.sigmoid(gate_pre)
    gate_grad = (
        act_grad * up_pre * sigmoid_gate * (1.0 + gate_pre * (1.0 - sigmoid_gate))
    ).astype(bf16)
    up_grad = (act_grad * gate_pre * sigmoid_gate).astype(bf16)
    pair_grad = jnp.concatenate([gate_grad, up_grad], axis=2)
    pair_weight = jnp.concatenate([gate_turned, up_turned], axis=2)

    far = jnp.einsum("esf,edf->esd", pair_grad, pair_weight[:, side:], preferred_element_type=f32)
    far = across_core(far.astype(bf16))
    near = jnp.einsum("esf,edf->esd", pair_grad, pair_weight[:, :side], preferred_element_type=f32)
    near = near + far.astype(f32)
    near = near[:, :, :share] + sum(
        along_x(near[:, :, k * share:(k + 1) * share].astype(bf16), k).astype(f32)
        for k in range(1, XN)
    )
    near = near.astype(bf16).reshape(own_experts, n_expert, capacity, share)
    near = near.transpose(1, 0, 2, 3).reshape(n_expert, own_experts * capacity, share)
    returned = lax.all_to_all(near, "expert", 0, 0, tiled=True)
    input_grad = wide_dot(
        pick.astype(bf16), returned.reshape(experts * capacity, share), ((0,), (0,))
    )

    head_blocks = wide_dot(normed_all, score_grad, ((0,), (0,)))
    head_grad = jnp.zeros((width, tile), f32)
    for at, start in enumerate(head_order):
        head_grad = lax.dynamic_update_slice_in_dim(
            head_grad, head_blocks[at * half:(at + 1) * half], start, 0
        )
    return (head_grad, residual_grad, input_grad)


def solution(mesh):
    in_specs = (
        P("expert", None),
        P("expert", None),
        P(),
        P(None, ("expert", "vocab")),
        P("expert"),
        P("expert"),
        P(),
        P("expert", None),
        P("expert", None),
        P("expert", None, "vocab"),
        P("expert", None, "vocab"),
        P("expert", "vocab", None),
    )
    out_specs = (P(None, ("expert", "vocab")), P("expert", "vocab"), P("expert", "vocab"))
    return jax.shard_map(
        on_device, mesh=mesh, in_specs=in_specs, out_specs=out_specs, check_vma=False
    )
```

```python
import math

import jax
import jax.numpy as jnp
from jax import lax
from jax.experimental import pallas as pl
from jax.experimental.pallas import tpu as pltpu
from jax.sharding import PartitionSpec as P

epsilon = 1e-05
YN, ZN, XN, CN = 4, 8, 4, 2
bf16 = jnp.bfloat16
f32 = jnp.float32


def wide_dot(a, b, dims, precision=None):
    return lax.dot_general(
        a, b, (dims, ((), ())), preferred_element_type=f32, precision=precision
    )


def along_y(a, step):
    moves = [
        (y * ZN + z, (y + step) % YN * ZN + z) for y in range(YN) for z in range(ZN)
    ]
    return lax.ppermute(a, "expert", moves)


def along_x(a, step):
    moves = [
        (x * CN + c, (x + step) % XN * CN + c) for x in range(XN) for c in range(CN)
    ]
    return lax.ppermute(a, "vocab", moves)


def across_core(a):
    moves = [(x * CN + c, x * CN + 1 - c) for x in range(XN) for c in range(CN)]
    return lax.ppermute(a, "vocab", moves)


def z_groups():
    return [[y * ZN + z for z in range(ZN)] for y in range(YN)]


def in_ring_order(a, move, ring):
    return [a] + [move(a, ring - k) for k in range(1, ring)]


def turned_weights(order, head_weight, w_gate, w_up, w_down):
    width, tile = head_weight.shape
    own, _, hidden = w_gate.shape
    count = order.shape[0]
    share = width // count

    def body(order_ref, head_ref, gate_ref, up_ref, down_ref, head_out, pair_out, down_out):
        head_out[...] = head_ref[...]
        pair_out[:, :, :hidden] = gate_ref[...]
        pair_out[:, :, hidden:] = up_ref[...]
        down_out[...] = down_ref[...]

    moved = 2 * (head_weight.size + 3 * w_gate.size)
    return pl.pallas_call(
        body,
        grid_spec=pltpu.PrefetchScalarGridSpec(
            num_scalar_prefetch=1,
            grid=(count,),
            in_specs=[
                pl.BlockSpec((share, tile), lambda i, s: (s[i], 0)),
                pl.BlockSpec((own, share, hidden), lambda i, s: (0, s[i], 0)),
                pl.BlockSpec((own, share, hidden), lambda i, s: (0, s[i], 0)),
                pl.BlockSpec((own, hidden, share), lambda i, s: (0, 0, s[i])),
            ],
            out_specs=[
                pl.BlockSpec((share, tile), lambda i, s: (i, 0)),
                pl.BlockSpec((own, share, 2 * hidden), lambda i, s: (0, i, 0)),
                pl.BlockSpec((own, hidden, share), lambda i, s: (0, 0, i)),
            ],
        ),
        out_shape=[
            jax.ShapeDtypeStruct((width, tile), bf16),
            jax.ShapeDtypeStruct((own, width, 2 * hidden), bf16),
            jax.ShapeDtypeStruct((own, hidden, width), bf16),
        ],
        cost_estimate=pl.CostEstimate(flops=0, bytes_accessed=2 * moved, transcendentals=0),
        name="turned_weights",
    )(order, head_weight, w_gate, w_up, w_down)


def head_gradient(order, near, far, score_grad):
    rows, side = near.shape
    tile = score_grad.shape[1]
    count = order.shape[0]
    share = 2 * side // count
    lead = count // 2

    def body(order_ref, near_ref, far_ref, grad_ref, out_ref):
        def product(rows_ref):
            out_ref[...] = wide_dot(rows_ref[...], grad_ref[...], ((0,), (0,)))

        @pl.when(pl.program_id(0) < lead)
        def _():
            product(near_ref)

        @pl.when(pl.program_id(0) >= lead)
        def _():
            product(far_ref)

    return pl.pallas_call(
        body,
        grid_spec=pltpu.PrefetchScalarGridSpec(
            num_scalar_prefetch=1,
            grid=(count,),
            in_specs=[
                pl.BlockSpec((rows, share), lambda i, s: (0, jnp.minimum(i, lead - 1))),
                pl.BlockSpec((rows, share), lambda i, s: (0, jnp.maximum(i - lead, 0))),
                pl.BlockSpec((rows, tile), lambda i, s: (0, 0)),
            ],
            out_specs=pl.BlockSpec((share, tile), lambda i, s: (s[i], 0)),
        ),
        out_shape=jax.ShapeDtypeStruct((2 * side, tile), f32),
        cost_estimate=pl.CostEstimate(
            flops=4 * rows * side * tile,
            bytes_accessed=4 * rows * side + 2 * rows * tile + 8 * side * tile,
            transcendentals=0,
        ),
        name="head_gradient",
    )(order, near, far, score_grad)


def on_device(
    layer_out,
    moe_input,
    final_gain,
    head_weight,
    clean_ids,
    levels,
    ratio_table,
    gate_weights,
    expert_ids,
    w_gate,
    w_up,
    w_down,
):
    rows, width = layer_out.shape
    n_expert = lax.axis_size("expert")
    n_vocab = lax.axis_size("vocab")
    all_rows = rows * n_expert
    own_experts = w_gate.shape[0]
    experts = own_experts * n_expert
    capacity = max(2, 2 * rows * expert_ids.shape[1] // experts)
    share = width // n_vocab
    half = share // 2
    tile = head_weight.shape[1]
    e_at = lax.axis_index("expert")
    v_at = lax.axis_index("vocab")
    y_at = e_at // ZN
    x_at, c_at = v_at // CN, v_at % CN

    order = jnp.stack(
        [
            ((x_at + k) % XN) * CN + (c_at + c) % CN
            for c in range(CN)
            for k in range(XN)
        ]
    )
    head_turned, pair_turned, down_turned = turned_weights(
        order, head_weight, w_gate, w_up, w_down
    )

    values = layer_out.astype(f32)
    row_scale = jnp.sqrt(jnp.mean(values * values, axis=1, keepdims=True) + epsilon)
    unit_share = (
        lax.dynamic_slice_in_dim(layer_out, v_at * share, share, 1).astype(f32) / row_scale
    )
    gain_share = lax.dynamic_slice_in_dim(final_gain, v_at * share, share, 0)[None, :]
    normed_share = (unit_share * gain_share).astype(bf16)

    labels = jnp.arange(experts, dtype=jnp.int32)
    hits = expert_ids[:, :, None] == labels
    naming = jnp.sum(hits.astype(f32), axis=1)
    before = (jnp.arange(rows)[:, None] > jnp.arange(rows)[None, :]).astype(f32)
    earlier = wide_dot(before, naming, ((1,), (0,)))
    gates = jnp.sum(jnp.where(hits, gate_weights[:, :, None], 0.0), axis=1)
    slots = jnp.arange(capacity, dtype=f32)
    taken = (earlier.T[:, None, :] == slots[None, :, None]) & (naming.T[:, None, :] > 0)
    slot_gate = jnp.sum(jnp.where(taken, gates.T[:, None, :], 0.0), axis=2)
    pick = taken.astype(f32).reshape(experts * capacity, rows)
    slot_gate = slot_gate.reshape(experts * capacity, 1)

    def by_expert(a):
        a = a.reshape(n_expert, own_experts, capacity, a.shape[-1])
        return a.transpose(1, 0, 2, 3).reshape(own_experts, n_expert * capacity, a.shape[-1])

    code = clean_ids * ratio_table.shape[0] + levels
    digits = jnp.stack([code % 256, code // 256 % 256, code // 65536]).astype(bf16)
    digits = jnp.pad(digits, ((0, 8 - digits.shape[0]), (0, share - rows)))
    along_z = lax.all_to_all(
        jnp.broadcast_to(
            jnp.concatenate([normed_share, digits], axis=0)[None], (ZN, rows + 8, share)
        ),
        "expert",
        0,
        0,
        axis_index_groups=z_groups(),
        tiled=True,
    )
    quarter = ZN * rows
    numbers = along_z[:, rows:, :half].reshape(ZN * 8, half)
    along_z = along_z[:, :rows].reshape(quarter, share)
    first = in_ring_order(
        jnp.concatenate([along_z[:, :half], numbers], axis=0), along_y, YN
    )
    second = jnp.concatenate(in_ring_order(along_z[:, half:], along_x, XN), axis=1)
    numbers = jnp.stack([a[quarter:] for a in first])
    first = jnp.concatenate([a[:quarter] for a in first], axis=0)
    first = in_ring_order(first, along_x, XN)
    second = jnp.concatenate(in_ring_order(second, along_y, YN), axis=0)
    normed_near = jnp.concatenate(
        [
            a
            for k in range(XN)
            for a in (first[k], second[:, k * half:(k + 1) * half])
        ],
        axis=1,
    )
    normed_far = across_core(normed_near)

    moe_share = lax.dynamic_slice_in_dim(moe_input, v_at * share, share, 1)
    inputs = wide_dot(pick.astype(bf16), moe_share, ((1,), (0,))).astype(bf16)
    inputs = lax.all_to_all(
        inputs.reshape(n_expert, own_experts * capacity, share), "expert", 0, 0, tiled=True
    )
    inputs = lax.all_gather(by_expert(inputs), "vocab", axis=2, tiled=True)

    side = width // 2
    numbers = numbers.reshape(YN, ZN, 8, half)[:, :, :3, :rows].astype(jnp.int32)
    code_all = numbers[:, :, 0] + 256 * numbers[:, :, 1] + 65536 * numbers[:, :, 2]
    code_all = code_all.reshape(all_rows, 1)
    clean_all = code_all // ratio_table.shape[0]
    level_all = code_all % ratio_table.shape[0]
    level_labels = jnp.arange(ratio_table.shape[0], dtype=jnp.int32)
    ratio_rows = jnp.sum(
        jnp.where(level_all == level_labels[None, :], ratio_table[None, :], 0.0),
        axis=1,
        keepdims=True,
    )
    columns = (e_at * n_vocab + v_at) * tile + jnp.arange(tile, dtype=jnp.int32)
    scores = wide_dot(normed_near, head_turned[:side], ((1,), (0,))) + wide_dot(
        normed_far, head_turned[side:], ((1,), (0,))
    )
    target_hit = (clean_all == columns[None, :]).astype(f32)
    loss_scale = 1.0 / math.sqrt(all_rows)
    score_grad = lax.optimization_barrier(
        ((jnp.exp(scores) - ratio_rows * target_hit) * loss_scale).astype(bf16)
    )
    head_grad = head_gradient(order, normed_near, normed_far, score_grad)

    far = wide_dot(score_grad, head_turned[side:], ((1,), (1,))).astype(bf16)
    far = across_core(far)
    near = wide_dot(score_grad, head_turned[:side], ((1,), (1,)))
    near = near + far.astype(f32)

    first = [near[:, k * share:k * share + half] for k in range(XN)]
    second = jnp.concatenate(
        [near[:, k * share + half:(k + 1) * share] for k in range(XN)], axis=1
    )
    first_sent = [along_x(first[k].astype(bf16), k) for k in range(1, XN)]
    second_sent = [
        along_y(second[i * quarter:(i + 1) * quarter].astype(bf16), i) for i in range(1, YN)
    ]
    first = first[0] + sum(a.astype(f32) for a in first_sent)
    second = second[:quarter] + sum(a.astype(f32) for a in second_sent)
    first, second, head_grad = lax.optimization_barrier((first, second, head_grad))
    first = first[:quarter] + sum(
        along_y(first[i * quarter:(i + 1) * quarter], i) for i in range(1, YN)
    )
    second = second[:, :half] + sum(
        along_x(second[:, k * half:(k + 1) * half], k) for k in range(1, XN)
    )
    gate_pre = jnp.einsum("esd,edf->esf", inputs, w_gate, preferred_element_type=f32)
    up_pre = jnp.einsum("esd,edf->esf", inputs, w_up, preferred_element_type=f32)
    first, second, gate_pre, up_pre = lax.optimization_barrier((first, second, gate_pre, up_pre))
    both = jnp.concatenate([first, second], axis=1).reshape(ZN, rows, share)
    normed_grad = jnp.sum(
        lax.all_to_all(both, "expert", 0, 0, axis_index_groups=z_groups(), tiled=True), axis=0
    )

    gained = gain_share * normed_grad
    total = jnp.sum(unit_share * gained, axis=1)
    total = total + across_core(total)
    total = total + sum(along_x(total, k) for k in range(1, XN))
    residual_grad = (gained - unit_share * (total / width)[:, None]) / row_scale

    routed = wide_dot(pick, residual_grad, ((1,), (0,)), lax.Precision.HIGHEST)
    routed = (slot_gate * routed).astype(bf16).reshape(n_expert, own_experts * capacity, share)
    routed = lax.all_to_all(routed, "expert", 0, 0, tiled=True)
    grads = jnp.concatenate(in_ring_order(by_expert(routed), along_x, XN), axis=2)
    grads_far = across_core(grads)

    act_grad = jnp.einsum(
        "esd,efd->esf", grads, down_turned[:, :, :side], preferred_element_type=f32
    ) + jnp.einsum(
        "esd,efd->esf", grads_far, down_turned[:, :, side:], preferred_element_type=f32
    )
    sigmoid_gate = jax.nn.sigmoid(gate_pre)
    gate_grad = (
        act_grad * up_pre * sigmoid_gate * (1.0 + gate_pre * (1.0 - sigmoid_gate))
    ).astype(bf16)
    up_grad = (act_grad * gate_pre * sigmoid_gate).astype(bf16)
    pair_grad = jnp.concatenate([gate_grad, up_grad], axis=2)

    far = jnp.einsum("esf,edf->esd", pair_grad, pair_turned[:, side:], preferred_element_type=f32)
    far = across_core(far.astype(bf16))
    near = jnp.einsum("esf,edf->esd", pair_grad, pair_turned[:, :side], preferred_element_type=f32)
    near = near + far.astype(f32)
    near = near[:, :, :share] + sum(
        along_x(near[:, :, k * share:(k + 1) * share].astype(bf16), k).astype(f32)
        for k in range(1, XN)
    )
    near = near.reshape(own_experts, n_expert, capacity, share)
    near = near.transpose(1, 0, 2, 3).reshape(n_expert, own_experts * capacity, share)
    returned = lax.all_to_all(near, "expert", 0, 0, tiled=True)
    input_grad = wide_dot(
        pick,
        returned.reshape(experts * capacity, share),
        ((0,), (0,)),
        lax.Precision.HIGHEST,
    )
    return (head_grad, residual_grad, input_grad)


def solution(mesh):
    in_specs = (
        P("expert", None),
        P("expert", None),
        P(),
        P(None, ("expert", "vocab")),
        P("expert"),
        P("expert"),
        P(),
        P("expert", None),
        P("expert", None),
        P("expert", None, "vocab"),
        P("expert", None, "vocab"),
        P("expert", "vocab", None),
    )
    out_specs = (P(None, ("expert", "vocab")), P("expert", "vocab"), P("expert", "vocab"))
    return jax.shard_map(
        on_device, mesh=mesh, in_specs=in_specs, out_specs=out_specs, check_vma=False
    )
```

```python
import math

import jax
import jax.numpy as jnp
from jax import lax
from jax.experimental import pallas as pl
from jax.experimental.pallas import tpu as pltpu
from jax.sharding import PartitionSpec as P

epsilon = 1e-05
YN, ZN, XN, CN = 4, 8, 4, 2
bf16 = jnp.bfloat16
f32 = jnp.float32


def wide_dot(a, b, dims, precision=None):
    return lax.dot_general(
        a, b, (dims, ((), ())), preferred_element_type=f32, precision=precision
    )


def along_y(a, step):
    moves = [
        (y * ZN + z, (y + step) % YN * ZN + z) for y in range(YN) for z in range(ZN)
    ]
    return lax.ppermute(a, "expert", moves)


def along_x(a, step):
    moves = [
        (x * CN + c, (x + step) % XN * CN + c) for x in range(XN) for c in range(CN)
    ]
    return lax.ppermute(a, "vocab", moves)


def across_core(a):
    moves = [(x * CN + c, x * CN + 1 - c) for x in range(XN) for c in range(CN)]
    return lax.ppermute(a, "vocab", moves)


def z_groups():
    return [[y * ZN + z for z in range(ZN)] for y in range(YN)]


def in_ring_order(a, move, ring):
    return [a] + [move(a, ring - k) for k in range(1, ring)]


def turned_weights(order, head_weight, w_gate, w_up, w_down):
    width, tile = head_weight.shape
    own, _, hidden = w_gate.shape
    count = order.shape[0]
    share = width // count

    def body(order_ref, head_ref, gate_ref, up_ref, down_ref, head_out, pair_out, down_out):
        head_out[...] = head_ref[...]
        pair_out[:, :, :hidden] = gate_ref[...]
        pair_out[:, :, hidden:] = up_ref[...]
        down_out[...] = down_ref[...]

    moved = 2 * (head_weight.size + 3 * w_gate.size)
    return pl.pallas_call(
        body,
        grid_spec=pltpu.PrefetchScalarGridSpec(
            num_scalar_prefetch=1,
            grid=(count,),
            in_specs=[
                pl.BlockSpec((share, tile), lambda i, s: (s[i], 0)),
                pl.BlockSpec((own, share, hidden), lambda i, s: (0, s[i], 0)),
                pl.BlockSpec((own, share, hidden), lambda i, s: (0, s[i], 0)),
                pl.BlockSpec((own, hidden, share), lambda i, s: (0, 0, s[i])),
            ],
            out_specs=[
                pl.BlockSpec((share, tile), lambda i, s: (i, 0)),
                pl.BlockSpec((own, share, 2 * hidden), lambda i, s: (0, i, 0)),
                pl.BlockSpec((own, hidden, share), lambda i, s: (0, 0, i)),
            ],
        ),
        out_shape=[
            jax.ShapeDtypeStruct((width, tile), bf16),
            jax.ShapeDtypeStruct((own, width, 2 * hidden), bf16),
            jax.ShapeDtypeStruct((own, hidden, width), bf16),
        ],
        cost_estimate=pl.CostEstimate(flops=0, bytes_accessed=2 * moved, transcendentals=0),
        name="turned_weights",
    )(order, head_weight, w_gate, w_up, w_down)


def head_gradient(order, near, far, score_grad):
    rows, side = near.shape
    tile = score_grad.shape[1]
    count = order.shape[0]
    share = 2 * side // count
    lead = count // 2

    def body(order_ref, near_ref, far_ref, grad_ref, out_ref):
        def product(rows_ref):
            out_ref[...] = wide_dot(rows_ref[...], grad_ref[...], ((0,), (0,)))

        @pl.when(pl.program_id(0) < lead)
        def _():
            product(near_ref)

        @pl.when(pl.program_id(0) >= lead)
        def _():
            product(far_ref)

    return pl.pallas_call(
        body,
        grid_spec=pltpu.PrefetchScalarGridSpec(
            num_scalar_prefetch=1,
            grid=(count,),
            in_specs=[
                pl.BlockSpec((rows, share), lambda i, s: (0, jnp.minimum(i, lead - 1))),
                pl.BlockSpec((rows, share), lambda i, s: (0, jnp.maximum(i - lead, 0))),
                pl.BlockSpec((rows, tile), lambda i, s: (0, 0)),
            ],
            out_specs=pl.BlockSpec((share, tile), lambda i, s: (s[i], 0)),
        ),
        out_shape=jax.ShapeDtypeStruct((2 * side, tile), f32),
        cost_estimate=pl.CostEstimate(
            flops=4 * rows * side * tile,
            bytes_accessed=4 * rows * side + 2 * rows * tile + 8 * side * tile,
            transcendentals=0,
        ),
        name="head_gradient",
    )(order, near, far, score_grad)


def laid_together(first, second):
    rows, half = first[0].shape
    part = second[0].shape[0]
    count = len(first)

    def body(*refs):
        out_ref = refs[-1]
        for k in range(count):
            out_ref[:, 2 * k * half:(2 * k + 1) * half] = refs[k][...]
            for i in range(count):
                out_ref[i * part:(i + 1) * part, (2 * k + 1) * half:(2 * k + 2) * half] = refs[
                    count + i
                ][:, k * half:(k + 1) * half]

    whole = pl.BlockSpec(memory_space=pltpu.VMEM)
    return pl.pallas_call(
        body,
        in_specs=[whole] * (2 * count),
        out_specs=whole,
        out_shape=jax.ShapeDtypeStruct((rows, 2 * count * half), bf16),
        cost_estimate=pl.CostEstimate(
            flops=0, bytes_accessed=8 * rows * count * half, transcendentals=0
        ),
        name="laid_together",
    )(*first, *second)


def near_gradient(score_grad, weight, far):
    rows, tile = score_grad.shape
    side = weight.shape[0]
    half = side // (2 * XN)
    part = rows // YN

    def body(grad_ref, weight_ref, far_ref, *outs):
        first = outs[:XN]
        second = outs[XN:]
        for i in range(YN):
            at = slice(i * part, (i + 1) * part)
            total = wide_dot(grad_ref[at, :], weight_ref[...], ((1,), (1,)))
            total = total + far_ref[at, :].astype(f32)
            for k in range(XN):
                low = 2 * k * half
                first[k][at, :] = total[:, low:low + half].astype(first[k].dtype)
                second[i][:, k * half:(k + 1) * half] = total[
                    :, low + half:low + 2 * half
                ].astype(second[i].dtype)

    whole = pl.BlockSpec(memory_space=pltpu.VMEM)
    kinds = [f32] + [bf16] * (XN - 1)
    outs = pl.pallas_call(
        body,
        in_specs=[whole] * 3,
        out_specs=[whole] * (XN + YN),
        out_shape=[jax.ShapeDtypeStruct((rows, half), t) for t in kinds]
        + [jax.ShapeDtypeStruct((part, XN * half), t) for t in kinds],
        cost_estimate=pl.CostEstimate(
            flops=2 * rows * tile * side, bytes_accessed=8 * rows * side, transcendentals=0
        ),
        compiler_params=pltpu.CompilerParams(vmem_limit_bytes=32 * 1024 * 1024),
        name="near_gradient",
    )(score_grad, weight, far)
    return outs[0], outs[XN], outs[1:XN], outs[XN + 1:]


def on_device(
    layer_out,
    moe_input,
    final_gain,
    head_weight,
    clean_ids,
    levels,
    ratio_table,
    gate_weights,
    expert_ids,
    w_gate,
    w_up,
    w_down,
):
    rows, width = layer_out.shape
    n_expert = lax.axis_size("expert")
    n_vocab = lax.axis_size("vocab")
    all_rows = rows * n_expert
    own_experts = w_gate.shape[0]
    experts = own_experts * n_expert
    capacity = max(2, 2 * rows * expert_ids.shape[1] // experts)
    share = width // n_vocab
    half = share // 2
    tile = head_weight.shape[1]
    e_at = lax.axis_index("expert")
    v_at = lax.axis_index("vocab")
    y_at = e_at // ZN
    x_at, c_at = v_at // CN, v_at % CN

    order = jnp.stack(
        [
            ((x_at + k) % XN) * CN + (c_at + c) % CN
            for c in range(CN)
            for k in range(XN)
        ]
    )
    head_turned, pair_turned, down_turned = turned_weights(
        order, head_weight, w_gate, w_up, w_down
    )

    values = layer_out.astype(f32)
    row_scale = jnp.sqrt(jnp.mean(values * values, axis=1, keepdims=True) + epsilon)
    unit_share = (
        lax.dynamic_slice_in_dim(layer_out, v_at * share, share, 1).astype(f32) / row_scale
    )
    gain_share = lax.dynamic_slice_in_dim(final_gain, v_at * share, share, 0)[None, :]
    normed_share = (unit_share * gain_share).astype(bf16)

    labels = jnp.arange(experts, dtype=jnp.int32)
    hits = expert_ids[:, :, None] == labels
    naming = jnp.sum(hits.astype(f32), axis=1)
    before = (jnp.arange(rows)[:, None] > jnp.arange(rows)[None, :]).astype(f32)
    earlier = wide_dot(before, naming, ((1,), (0,)))
    gates = jnp.sum(jnp.where(hits, gate_weights[:, :, None], 0.0), axis=1)
    slots = jnp.arange(capacity, dtype=f32)
    taken = (earlier.T[:, None, :] == slots[None, :, None]) & (naming.T[:, None, :] > 0)
    slot_gate = jnp.sum(jnp.where(taken, gates.T[:, None, :], 0.0), axis=2)
    pick = taken.astype(f32).reshape(experts * capacity, rows)
    slot_gate = slot_gate.reshape(experts * capacity, 1)

    def by_expert(a):
        a = a.reshape(n_expert, own_experts, capacity, a.shape[-1])
        return a.transpose(1, 0, 2, 3).reshape(own_experts, n_expert * capacity, a.shape[-1])

    moe_share = lax.dynamic_slice_in_dim(moe_input, v_at * share, share, 1)
    inputs = wide_dot(pick.astype(bf16), moe_share, ((1,), (0,))).astype(bf16)
    inputs = inputs.reshape(n_expert, own_experts * capacity, share)

    code = clean_ids * ratio_table.shape[0] + levels
    digits = jnp.stack([code % 256, code // 256 % 256, code // 65536]).astype(bf16)
    digits = jnp.pad(digits, ((0, 8 - digits.shape[0]), (0, share - rows)))
    along_z = lax.all_to_all(
        jnp.broadcast_to(
            jnp.concatenate([normed_share, digits], axis=0)[None], (ZN, rows + 8, share)
        ),
        "expert",
        0,
        0,
        axis_index_groups=z_groups(),
        tiled=True,
    )
    along_z, head_turned, pair_turned, down_turned, inputs, pick, slot_gate = (
        lax.optimization_barrier(
            (along_z, head_turned, pair_turned, down_turned, inputs, pick, slot_gate)
        )
    )
    quarter = ZN * rows
    numbers = along_z[:, rows:, :half].reshape(ZN * 8, half)
    along_z = along_z[:, :rows].reshape(quarter, share)
    first, second = lax.optimization_barrier(
        (jnp.concatenate([along_z[:, :half], numbers], axis=0), along_z[:, half:])
    )
    first = in_ring_order(first, along_y, YN)
    second = jnp.concatenate(in_ring_order(second, along_x, XN), axis=1)
    numbers = jnp.stack([a[quarter:] for a in first])
    first = jnp.concatenate([a[:quarter] for a in first], axis=0)
    first, second, numbers, inputs = lax.optimization_barrier((first, second, numbers, inputs))
    first = in_ring_order(first, along_x, XN)
    second = in_ring_order(second, along_y, YN)
    inputs = lax.all_to_all(inputs, "expert", 0, 0, tiled=True)
    first, second, inputs = lax.optimization_barrier((first, second, inputs))
    normed_near = laid_together(first, second)
    normed_far = across_core(normed_near)

    inputs = lax.all_gather(by_expert(inputs), "vocab", axis=2, tiled=True)

    side = width // 2
    numbers = numbers.reshape(YN, ZN, 8, half)[:, :, :3, :rows].astype(jnp.int32)
    code_all = numbers[:, :, 0] + 256 * numbers[:, :, 1] + 65536 * numbers[:, :, 2]
    code_all = code_all.reshape(all_rows, 1)
    clean_all = code_all // ratio_table.shape[0]
    level_all = code_all % ratio_table.shape[0]
    level_labels = jnp.arange(ratio_table.shape[0], dtype=jnp.int32)
    ratio_rows = jnp.sum(
        jnp.where(level_all == level_labels[None, :], ratio_table[None, :], 0.0),
        axis=1,
        keepdims=True,
    )
    columns = (e_at * n_vocab + v_at) * tile + jnp.arange(tile, dtype=jnp.int32)
    scores = wide_dot(normed_near, head_turned[:side], ((1,), (0,))) + wide_dot(
        normed_far, head_turned[side:], ((1,), (0,))
    )
    target_hit = (clean_all == columns[None, :]).astype(f32)
    loss_scale = 1.0 / math.sqrt(all_rows)
    score_grad = lax.optimization_barrier(
        ((jnp.exp(scores) - ratio_rows * target_hit) * loss_scale).astype(bf16)
    )
    far = wide_dot(score_grad, head_turned[side:], ((1,), (1,))).astype(bf16)
    far = across_core(far)
    first, second, first_sent, second_sent = near_gradient(
        score_grad, head_turned[:side], far
    )
    first, second, first_sent, second_sent, score_grad, inputs = lax.optimization_barrier(
        (first, second, first_sent, second_sent, score_grad, inputs)
    )
    first_sent = [along_x(a, k + 1) for k, a in enumerate(first_sent)]
    second_sent = [along_y(a, i + 1) for i, a in enumerate(second_sent)]
    head_grad = head_gradient(order, normed_near, normed_far, score_grad)
    gate_pre = jnp.einsum("esd,edf->esf", inputs, w_gate, preferred_element_type=f32)
    up_pre = jnp.einsum("esd,edf->esf", inputs, w_up, preferred_element_type=f32)
    first_sent, second_sent, head_grad, gate_pre, up_pre = lax.optimization_barrier(
        (first_sent, second_sent, head_grad, gate_pre, up_pre)
    )
    first = first + sum(a.astype(f32) for a in first_sent)
    second = second + sum(a.astype(f32) for a in second_sent)
    first_sent = [first[i * quarter:(i + 1) * quarter] for i in range(1, YN)]
    second_sent = [second[:, k * half:(k + 1) * half] for k in range(1, XN)]
    first, second, first_sent, second_sent = lax.optimization_barrier(
        (first[:quarter], second[:, :half], first_sent, second_sent)
    )
    first = first + sum(along_y(a, i + 1) for i, a in enumerate(first_sent))
    second = second + sum(along_x(a, k + 1) for k, a in enumerate(second_sent))
    both = jnp.concatenate([first, second], axis=1).reshape(ZN, rows, share)
    normed_grad = jnp.sum(
        lax.all_to_all(both, "expert", 0, 0, axis_index_groups=z_groups(), tiled=True), axis=0
    )

    gained = gain_share * normed_grad
    total = jnp.sum(unit_share * gained, axis=1)
    total = total + across_core(total)
    total = total + sum(along_x(total, k) for k in range(1, XN))
    residual_grad = (gained - unit_share * (total / width)[:, None]) / row_scale

    routed = wide_dot(pick, residual_grad, ((1,), (0,)), lax.Precision.HIGHEST)
    routed = (slot_gate * routed).astype(bf16).reshape(n_expert, own_experts * capacity, share)
    routed = lax.all_to_all(routed, "expert", 0, 0, tiled=True)
    grads = jnp.concatenate(in_ring_order(by_expert(routed), along_x, XN), axis=2)
    grads_far = across_core(grads)

    act_grad = jnp.einsum(
        "esd,efd->esf", grads, down_turned[:, :, :side], preferred_element_type=f32
    ) + jnp.einsum(
        "esd,efd->esf", grads_far, down_turned[:, :, side:], preferred_element_type=f32
    )
    sigmoid_gate = jax.nn.sigmoid(gate_pre)
    gate_grad = (
        act_grad * up_pre * sigmoid_gate * (1.0 + gate_pre * (1.0 - sigmoid_gate))
    ).astype(bf16)
    up_grad = (act_grad * gate_pre * sigmoid_gate).astype(bf16)
    pair_grad = jnp.concatenate([gate_grad, up_grad], axis=2)

    far = jnp.einsum("esf,edf->esd", pair_grad, pair_turned[:, side:], preferred_element_type=f32)
    far = across_core(far.astype(bf16))
    near = jnp.einsum("esf,edf->esd", pair_grad, pair_turned[:, :side], preferred_element_type=f32)
    near = near + far.astype(f32)
    near = near[:, :, :share] + sum(
        along_x(near[:, :, k * share:(k + 1) * share].astype(bf16), k).astype(f32)
        for k in range(1, XN)
    )
    near = near.reshape(own_experts, n_expert, capacity, share)
    near = near.transpose(1, 0, 2, 3).reshape(n_expert, own_experts * capacity, share)
    returned = lax.all_to_all(near, "expert", 0, 0, tiled=True)
    input_grad = wide_dot(
        pick,
        returned.reshape(experts * capacity, share),
        ((0,), (0,)),
        lax.Precision.HIGHEST,
    )
    return (head_grad, residual_grad, input_grad)


def solution(mesh):
    in_specs = (
        P("expert", None),
        P("expert", None),
        P(),
        P(None, ("expert", "vocab")),
        P("expert"),
        P("expert"),
        P(),
        P("expert", None),
        P("expert", None),
        P("expert", None, "vocab"),
        P("expert", None, "vocab"),
        P("expert", "vocab", None),
    )
    out_specs = (P(None, ("expert", "vocab")), P("expert", "vocab"), P("expert", "vocab"))
    return jax.shard_map(
        on_device, mesh=mesh, in_specs=in_specs, out_specs=out_specs, check_vma=False
    )
```

```python
import math

import jax
import jax.numpy as jnp
from jax import lax
from jax.experimental import pallas as pl
from jax.experimental.pallas import tpu as pltpu
from jax.sharding import Mesh, PartitionSpec as P

epsilon = 1e-05
YN, ZN, XN, CN = 4, 8, 4, 2
bf16 = jnp.bfloat16
f32 = jnp.float32


def wide_dot(a, b, dims, precision=None):
    return lax.dot_general(
        a, b, (dims, ((), ())), preferred_element_type=f32, precision=precision
    )


def along_y(a, step):
    return lax.ppermute(a, "y", [(p, (p + step) % YN) for p in range(YN)])


def along_x(a, step):
    return lax.ppermute(a, "x", [(p, (p + step) % XN) for p in range(XN)])


def across_core(a):
    return lax.ppermute(a, "core", [(p, CN - 1 - p) for p in range(CN)])


def exchanged(a, axes):
    return lax.all_to_all(a, axes, 0, 0, tiled=True)


def in_ring_order(a, move, ring):
    return [a] + [move(a, ring - k) for k in range(1, ring)]


def turned_weights(order, head_weight, w_gate, w_up, w_down):
    width, tile = head_weight.shape
    own, _, hidden = w_gate.shape
    count = order.shape[0]
    share = width // count

    def body(order_ref, head_ref, gate_ref, up_ref, down_ref, head_out, pair_out, down_out):
        head_out[...] = head_ref[...]
        pair_out[:, :, :hidden] = gate_ref[...]
        pair_out[:, :, hidden:] = up_ref[...]
        down_out[...] = down_ref[...]

    moved = 2 * (head_weight.size + 3 * w_gate.size)
    return pl.pallas_call(
        body,
        grid_spec=pltpu.PrefetchScalarGridSpec(
            num_scalar_prefetch=1,
            grid=(count,),
            in_specs=[
                pl.BlockSpec((share, tile), lambda i, s: (s[i], 0)),
                pl.BlockSpec((own, share, hidden), lambda i, s: (0, s[i], 0)),
                pl.BlockSpec((own, share, hidden), lambda i, s: (0, s[i], 0)),
                pl.BlockSpec((own, hidden, share), lambda i, s: (0, 0, s[i])),
            ],
            out_specs=[
                pl.BlockSpec((share, tile), lambda i, s: (i, 0)),
                pl.BlockSpec((own, share, 2 * hidden), lambda i, s: (0, i, 0)),
                pl.BlockSpec((own, hidden, share), lambda i, s: (0, 0, i)),
            ],
        ),
        out_shape=[
            jax.ShapeDtypeStruct((width, tile), bf16),
            jax.ShapeDtypeStruct((own, width, 2 * hidden), bf16),
            jax.ShapeDtypeStruct((own, hidden, width), bf16),
        ],
        cost_estimate=pl.CostEstimate(flops=0, bytes_accessed=2 * moved, transcendentals=0),
        name="turned_weights",
    )(order, head_weight, w_gate, w_up, w_down)


def head_gradient(order, near, far, score_grad):
    rows, side = near.shape
    tile = score_grad.shape[1]
    count = order.shape[0]
    share = 2 * side // count
    lead = count // 2

    def body(order_ref, near_ref, far_ref, grad_ref, out_ref):
        def product(rows_ref):
            out_ref[...] = wide_dot(rows_ref[...], grad_ref[...], ((0,), (0,)))

        @pl.when(pl.program_id(0) < lead)
        def _():
            product(near_ref)

        @pl.when(pl.program_id(0) >= lead)
        def _():
            product(far_ref)

    return pl.pallas_call(
        body,
        grid_spec=pltpu.PrefetchScalarGridSpec(
            num_scalar_prefetch=1,
            grid=(count,),
            in_specs=[
                pl.BlockSpec((rows, share), lambda i, s: (0, jnp.minimum(i, lead - 1))),
                pl.BlockSpec((rows, share), lambda i, s: (0, jnp.maximum(i - lead, 0))),
                pl.BlockSpec((rows, tile), lambda i, s: (0, 0)),
            ],
            out_specs=pl.BlockSpec((share, tile), lambda i, s: (s[i], 0)),
        ),
        out_shape=jax.ShapeDtypeStruct((2 * side, tile), f32),
        cost_estimate=pl.CostEstimate(
            flops=4 * rows * side * tile,
            bytes_accessed=4 * rows * side + 2 * rows * tile + 8 * side * tile,
            transcendentals=0,
        ),
        name="head_gradient",
    )(order, near, far, score_grad)


def near_gradient(score_grad, weight, far):
    rows, tile = score_grad.shape
    share = weight.shape[0] // XN
    part = rows // YN

    def body(grad_ref, weight_ref, far_ref, *outs):
        for k in range(XN):
            low = slice(k * share, (k + 1) * share)
            for i in range(YN):
                at = slice(i * part, (i + 1) * part)
                total = wide_dot(grad_ref[at, :], weight_ref[low, :], ((1,), (1,)))
                total = total + far_ref[at, low].astype(f32)
                outs[k][at, :] = total.astype(outs[k].dtype)

    whole = pl.BlockSpec(memory_space=pltpu.VMEM)
    return pl.pallas_call(
        body,
        in_specs=[whole] * 3,
        out_specs=[whole] * XN,
        out_shape=[
            jax.ShapeDtypeStruct((rows, share), t) for t in [f32] + [bf16] * (XN - 1)
        ],
        cost_estimate=pl.CostEstimate(
            flops=2 * rows * tile * share * XN,
            bytes_accessed=8 * rows * share * XN,
            transcendentals=0,
        ),
        compiler_params=pltpu.CompilerParams(vmem_limit_bytes=32 * 1024 * 1024),
        name="near_gradient",
    )(score_grad, weight, far)


def on_device(
    layer_out,
    moe_input,
    final_gain,
    head_weight,
    clean_ids,
    levels,
    ratio_table,
    gate_weights,
    expert_ids,
    w_gate,
    w_up,
    w_down,
):
    rows, width = layer_out.shape
    n_expert = YN * ZN
    n_vocab = XN * CN
    all_rows = rows * n_expert
    own_experts = w_gate.shape[0]
    experts = own_experts * n_expert
    capacity = max(2, 2 * rows * expert_ids.shape[1] // experts)
    share = width // n_vocab
    tile = head_weight.shape[1]
    y_at, x_at, c_at = lax.axis_index("y"), lax.axis_index("x"), lax.axis_index("core")
    e_at = y_at * ZN + lax.axis_index("z")
    v_at = x_at * CN + c_at

    order = jnp.stack(
        [((x_at + k) % XN) * CN + (c_at + c) % CN for c in range(CN) for k in range(XN)]
    )
    head_turned, pair_turned, down_turned = turned_weights(
        order, head_weight, w_gate, w_up, w_down
    )

    values = layer_out.astype(f32)
    row_scale = jnp.sqrt(jnp.mean(values * values, axis=1, keepdims=True) + epsilon)
    unit_share = (
        lax.dynamic_slice_in_dim(layer_out, v_at * share, share, 1).astype(f32) / row_scale
    )
    gain_share = lax.dynamic_slice_in_dim(final_gain, v_at * share, share, 0)[None, :]
    normed_share = (unit_share * gain_share).astype(bf16)

    labels = jnp.arange(experts, dtype=jnp.int32)
    hits = expert_ids[:, :, None] == labels
    naming = jnp.sum(hits.astype(f32), axis=1)
    before = (jnp.arange(rows)[:, None] > jnp.arange(rows)[None, :]).astype(f32)
    earlier = wide_dot(before, naming, ((1,), (0,)))
    gates = jnp.sum(jnp.where(hits, gate_weights[:, :, None], 0.0), axis=1)
    slots = jnp.arange(capacity, dtype=f32)
    taken = (earlier.T[:, None, :] == slots[None, :, None]) & (naming.T[:, None, :] > 0)
    slot_gate = jnp.sum(jnp.where(taken, gates.T[:, None, :], 0.0), axis=2)
    pick = taken.astype(f32).reshape(experts * capacity, rows)
    slot_gate = slot_gate.reshape(experts * capacity, 1)

    def by_expert(a):
        a = a.reshape(n_expert, own_experts, capacity, a.shape[-1])
        return a.transpose(1, 0, 2, 3).reshape(own_experts, n_expert * capacity, a.shape[-1])

    moe_share = lax.dynamic_slice_in_dim(moe_input, v_at * share, share, 1)
    inputs = wide_dot(pick.astype(bf16), moe_share, ((1,), (0,))).astype(bf16)
    inputs = inputs.reshape(n_expert, own_experts * capacity, share)

    code = clean_ids * ratio_table.shape[0] + levels
    digits = jnp.stack([code % 256, code // 256 % 256, code // 65536]).astype(bf16)
    digits = jnp.pad(digits, ((0, 8 - digits.shape[0]), (0, share - rows)))
    spread = jnp.broadcast_to(
        jnp.concatenate([normed_share, digits], axis=0)[None], (n_expert, rows + 8, share)
    )
    spread = exchanged(spread, ("y", "z"))
    spread, head_turned, pair_turned, down_turned, inputs, pick, slot_gate = (
        lax.optimization_barrier(
            (spread, head_turned, pair_turned, down_turned, inputs, pick, slot_gate)
        )
    )
    numbers = spread[:, rows:]
    normed_near = in_ring_order(spread[:, :rows].reshape(all_rows, share), along_x, XN)
    inputs = exchanged(inputs, ("y", "z"))
    normed_near, inputs = lax.optimization_barrier((normed_near, inputs))
    normed_near = jnp.concatenate(normed_near, axis=1)
    normed_far = across_core(normed_near)

    inputs = lax.all_gather(by_expert(inputs), ("x", "core"), axis=2, tiled=True)

    side = width // 2
    numbers = numbers[:, :3, :rows].astype(jnp.int32)
    code_all = numbers[:, 0] + 256 * numbers[:, 1] + 65536 * numbers[:, 2]
    code_all = code_all.reshape(all_rows, 1)
    clean_all = code_all // ratio_table.shape[0]
    level_all = code_all % ratio_table.shape[0]
    level_labels = jnp.arange(ratio_table.shape[0], dtype=jnp.int32)
    ratio_rows = jnp.sum(
        jnp.where(level_all == level_labels[None, :], ratio_table[None, :], 0.0),
        axis=1,
        keepdims=True,
    )
    columns = (e_at * n_vocab + v_at) * tile + jnp.arange(tile, dtype=jnp.int32)
    scores = wide_dot(normed_near, head_turned[:side], ((1,), (0,))) + wide_dot(
        normed_far, head_turned[side:], ((1,), (0,))
    )
    target_hit = (clean_all == columns[None, :]).astype(f32)
    loss_scale = 1.0 / math.sqrt(all_rows)
    score_grad = lax.optimization_barrier(
        ((jnp.exp(scores) - ratio_rows * target_hit) * loss_scale).astype(bf16)
    )
    far = wide_dot(score_grad, head_turned[side:], ((1,), (1,))).astype(bf16)
    far = across_core(far)
    kept, *sent = near_gradient(score_grad, head_turned[:side], far)
    kept, sent, score_grad = lax.optimization_barrier((kept, sent, score_grad))
    sent = [along_x(a, k + 1) for k, a in enumerate(sent)]
    head_grad = head_gradient(order, normed_near, normed_far, score_grad)
    inputs, head_grad = lax.optimization_barrier((inputs, head_grad))
    gate_pre = jnp.einsum("esd,edf->esf", inputs, w_gate, preferred_element_type=f32)
    up_pre = jnp.einsum("esd,edf->esf", inputs, w_up, preferred_element_type=f32)
    sent, head_grad, gate_pre, up_pre = lax.optimization_barrier(
        (sent, head_grad, gate_pre, up_pre)
    )
    kept = kept + sum(a.astype(f32) for a in sent)
    kept = exchanged(kept.reshape(n_expert, rows, share), ("y", "z"))
    normed_grad = jnp.sum(kept, axis=0)

    gained = gain_share * normed_grad
    total = jnp.sum(unit_share * gained, axis=1)
    total = total + across_core(total)
    total = total + sum(along_x(total, k) for k in range(1, XN))
    residual_grad = (gained - unit_share * (total / width)[:, None]) / row_scale

    routed = wide_dot(pick, residual_grad, ((1,), (0,)), lax.Precision.HIGHEST)
    routed = (slot_gate * routed).astype(bf16).reshape(n_expert, own_experts * capacity, share)
    routed = lax.all_to_all(routed, ("y", "z"), 0, 0, tiled=True)
    grads = jnp.concatenate(in_ring_order(by_expert(routed), along_x, XN), axis=2)
    grads_far = across_core(grads)

    act_grad = jnp.einsum(
        "esd,efd->esf", grads, down_turned[:, :, :side], preferred_element_type=f32
    ) + jnp.einsum(
        "esd,efd->esf", grads_far, down_turned[:, :, side:], preferred_element_type=f32
    )
    sigmoid_gate = jax.nn.sigmoid(gate_pre)
    gate_grad = (
        act_grad * up_pre * sigmoid_gate * (1.0 + gate_pre * (1.0 - sigmoid_gate))
    ).astype(bf16)
    up_grad = (act_grad * gate_pre * sigmoid_gate).astype(bf16)
    pair_grad = jnp.concatenate([gate_grad, up_grad], axis=2)

    far = jnp.einsum("esf,edf->esd", pair_grad, pair_turned[:, side:], preferred_element_type=f32)
    far = across_core(far.astype(bf16))
    near = jnp.einsum("esf,edf->esd", pair_grad, pair_turned[:, :side], preferred_element_type=f32)
    near = near + far.astype(f32)
    near = near[:, :, :share] + sum(
        along_x(near[:, :, k * share:(k + 1) * share].astype(bf16), k).astype(f32)
        for k in range(1, XN)
    )
    near = near.reshape(own_experts, n_expert, capacity, share)
    near = near.transpose(1, 0, 2, 3).reshape(n_expert, own_experts * capacity, share)
    returned = lax.all_to_all(near, ("y", "z"), 0, 0, tiled=True)
    input_grad = wide_dot(
        pick,
        returned.reshape(experts * capacity, share),
        ((0,), (0,)),
        lax.Precision.HIGHEST,
    )
    return (head_grad, residual_grad, input_grad)


def solution(mesh):
    fine = Mesh(mesh.devices.reshape(YN, ZN, XN, CN), ("y", "z", "x", "core"))
    expert, vocab = ("y", "z"), ("x", "core")
    everywhere = expert + vocab
    in_specs = (
        P(expert, None),
        P(expert, None),
        P(),
        P(None, everywhere),
        P(expert),
        P(expert),
        P(),
        P(expert, None),
        P(expert, None),
        P(expert, None, vocab),
        P(expert, None, vocab),
        P(expert, vocab, None),
    )
    out_specs = (P(None, everywhere), P(expert, vocab), P(expert, vocab))
    return jax.shard_map(
        on_device, mesh=fine, in_specs=in_specs, out_specs=out_specs, check_vma=False
    )
```

```python
import math

import jax
import jax.numpy as jnp
from jax import lax
from jax.experimental import pallas as pl
from jax.experimental.pallas import tpu as pltpu
from jax.sharding import Mesh, PartitionSpec as P

epsilon = 1e-05
YN, ZN, XN, CN = 4, 8, 4, 2
bf16 = jnp.bfloat16
f32 = jnp.float32


def wide_dot(a, b, dims, precision=None):
    return lax.dot_general(
        a, b, (dims, ((), ())), preferred_element_type=f32, precision=precision
    )


def along_y(a, step):
    return lax.ppermute(a, "y", [(p, (p + step) % YN) for p in range(YN)])


def along_x(a, step):
    return lax.ppermute(a, "x", [(p, (p + step) % XN) for p in range(XN)])


def across_core(a):
    return lax.ppermute(a, "core", [(p, CN - 1 - p) for p in range(CN)])


def exchanged(a, axes):
    return lax.all_to_all(a, axes, 0, 0, tiled=True)


def in_ring_order(a, move, ring):
    return [a] + [move(a, ring - k) for k in range(1, ring)]


def turned_weights(order, head_weight, w_gate, w_up, w_down):
    width, tile = head_weight.shape
    own, _, hidden = w_gate.shape
    count = order.shape[0]
    share = width // count

    def body(order_ref, head_ref, gate_ref, up_ref, down_ref, head_out, pair_out, down_out):
        head_out[...] = head_ref[...]
        pair_out[:, :, :hidden] = gate_ref[...]
        pair_out[:, :, hidden:] = up_ref[...]
        down_out[...] = down_ref[...]

    moved = 2 * (head_weight.size + 3 * w_gate.size)
    return pl.pallas_call(
        body,
        grid_spec=pltpu.PrefetchScalarGridSpec(
            num_scalar_prefetch=1,
            grid=(count,),
            in_specs=[
                pl.BlockSpec((share, tile), lambda i, s: (s[i], 0)),
                pl.BlockSpec((own, share, hidden), lambda i, s: (0, s[i], 0)),
                pl.BlockSpec((own, share, hidden), lambda i, s: (0, s[i], 0)),
                pl.BlockSpec((own, hidden, share), lambda i, s: (0, 0, s[i])),
            ],
            out_specs=[
                pl.BlockSpec((share, tile), lambda i, s: (i, 0)),
                pl.BlockSpec((own, share, 2 * hidden), lambda i, s: (0, i, 0)),
                pl.BlockSpec((own, hidden, share), lambda i, s: (0, 0, i)),
            ],
        ),
        out_shape=[
            jax.ShapeDtypeStruct((width, tile), bf16),
            jax.ShapeDtypeStruct((own, width, 2 * hidden), bf16),
            jax.ShapeDtypeStruct((own, hidden, width), bf16),
        ],
        cost_estimate=pl.CostEstimate(flops=0, bytes_accessed=2 * moved, transcendentals=0),
        name="turned_weights",
    )(order, head_weight, w_gate, w_up, w_down)


def head_gradient(order, near, far, score_grad):
    rows, side = near.shape
    tile = score_grad.shape[1]
    count = order.shape[0]
    share = 2 * side // count
    lead = count // 2

    def body(order_ref, near_ref, far_ref, grad_ref, out_ref):
        def product(rows_ref):
            out_ref[...] = wide_dot(rows_ref[...], grad_ref[...], ((0,), (0,)))

        @pl.when(pl.program_id(0) < lead)
        def _():
            product(near_ref)

        @pl.when(pl.program_id(0) >= lead)
        def _():
            product(far_ref)

    return pl.pallas_call(
        body,
        grid_spec=pltpu.PrefetchScalarGridSpec(
            num_scalar_prefetch=1,
            grid=(count,),
            in_specs=[
                pl.BlockSpec((rows, share), lambda i, s: (0, jnp.minimum(i, lead - 1))),
                pl.BlockSpec((rows, share), lambda i, s: (0, jnp.maximum(i - lead, 0))),
                pl.BlockSpec((rows, tile), lambda i, s: (0, 0)),
            ],
            out_specs=pl.BlockSpec((share, tile), lambda i, s: (s[i], 0)),
        ),
        out_shape=jax.ShapeDtypeStruct((2 * side, tile), f32),
        cost_estimate=pl.CostEstimate(flops=1024, bytes_accessed=1024, transcendentals=0),
        name="head_gradient",
    )(order, near, far, score_grad)


def near_gradient(score_grad, weight, far):
    rows, tile = score_grad.shape
    share = weight.shape[0] // XN
    part = rows // YN

    def body(grad_ref, weight_ref, far_ref, *outs):
        for k in range(XN):
            low = slice(k * share, (k + 1) * share)
            for i in range(YN):
                at = slice(i * part, (i + 1) * part)
                total = wide_dot(grad_ref[at, :], weight_ref[low, :], ((1,), (1,)))
                total = total + far_ref[at, low].astype(f32)
                outs[k][at, :] = total.astype(outs[k].dtype)

    whole = pl.BlockSpec(memory_space=pltpu.VMEM)
    return pl.pallas_call(
        body,
        in_specs=[whole] * 3,
        out_specs=[whole] * XN,
        out_shape=[
            jax.ShapeDtypeStruct((rows, share), t) for t in [f32] + [bf16] * (XN - 1)
        ],
        cost_estimate=pl.CostEstimate(
            flops=2 * rows * tile * share * XN,
            bytes_accessed=8 * rows * share * XN,
            transcendentals=0,
        ),
        compiler_params=pltpu.CompilerParams(vmem_limit_bytes=32 * 1024 * 1024),
        name="near_gradient",
    )(score_grad, weight, far)


def on_device(
    layer_out,
    moe_input,
    final_gain,
    head_weight,
    clean_ids,
    levels,
    ratio_table,
    gate_weights,
    expert_ids,
    w_gate,
    w_up,
    w_down,
):
    rows, width = layer_out.shape
    n_expert = YN * ZN
    n_vocab = XN * CN
    all_rows = rows * n_expert
    own_experts = w_gate.shape[0]
    experts = own_experts * n_expert
    capacity = max(2, 2 * rows * expert_ids.shape[1] // experts)
    share = width // n_vocab
    tile = head_weight.shape[1]
    y_at, x_at, c_at = lax.axis_index("y"), lax.axis_index("x"), lax.axis_index("core")
    e_at = y_at * ZN + lax.axis_index("z")
    v_at = x_at * CN + c_at

    order = jnp.stack(
        [((x_at + k) % XN) * CN + (c_at + c) % CN for c in range(CN) for k in range(XN)]
    )
    head_turned, pair_turned, down_turned = turned_weights(
        order, head_weight, w_gate, w_up, w_down
    )

    values = layer_out.astype(f32)
    row_scale = jnp.sqrt(jnp.mean(values * values, axis=1, keepdims=True) + epsilon)
    unit_share = (
        lax.dynamic_slice_in_dim(layer_out, v_at * share, share, 1).astype(f32) / row_scale
    )
    gain_share = lax.dynamic_slice_in_dim(final_gain, v_at * share, share, 0)[None, :]
    normed_share = (unit_share * gain_share).astype(bf16)

    labels = jnp.arange(experts, dtype=jnp.int32)
    hits = expert_ids[:, :, None] == labels
    naming = jnp.sum(hits.astype(f32), axis=1)
    before = (jnp.arange(rows)[:, None] > jnp.arange(rows)[None, :]).astype(f32)
    earlier = wide_dot(before, naming, ((1,), (0,)))
    gates = jnp.sum(jnp.where(hits, gate_weights[:, :, None], 0.0), axis=1)
    slots = jnp.arange(capacity, dtype=f32)
    taken = (earlier.T[:, None, :] == slots[None, :, None]) & (naming.T[:, None, :] > 0)
    slot_gate = jnp.sum(jnp.where(taken, gates.T[:, None, :], 0.0), axis=2)
    pick = taken.astype(f32).reshape(experts * capacity, rows)
    slot_gate = slot_gate.reshape(experts * capacity, 1)

    def by_expert(a):
        a = a.reshape(n_expert, own_experts, capacity, a.shape[-1])
        return a.transpose(1, 0, 2, 3).reshape(own_experts, n_expert * capacity, a.shape[-1])

    moe_share = lax.dynamic_slice_in_dim(moe_input, v_at * share, share, 1)
    inputs = wide_dot(pick.astype(bf16), moe_share, ((1,), (0,))).astype(bf16)
    inputs = inputs.reshape(n_expert, own_experts * capacity, share)

    code = clean_ids * ratio_table.shape[0] + levels
    digits = jnp.stack([code % 256, code // 256 % 256, code // 65536]).astype(bf16)
    digits = jnp.pad(digits, ((0, 8 - digits.shape[0]), (0, share - rows)))
    spread = jnp.broadcast_to(
        jnp.concatenate([normed_share, digits], axis=0)[None], (n_expert, rows + 8, share)
    )
    spread = exchanged(spread, ("y", "z"))
    spread, head_turned, pair_turned, down_turned, inputs, pick, slot_gate = (
        lax.optimization_barrier(
            (spread, head_turned, pair_turned, down_turned, inputs, pick, slot_gate)
        )
    )
    numbers = spread[:, rows:]
    normed_near = in_ring_order(spread[:, :rows].reshape(all_rows, share), along_x, XN)
    inputs = exchanged(inputs, ("y", "z"))
    normed_near, inputs = lax.optimization_barrier((normed_near, inputs))
    normed_near = jnp.concatenate(normed_near, axis=1)
    normed_far = across_core(normed_near)

    inputs = lax.all_gather(by_expert(inputs), ("x", "core"), axis=2, tiled=True)

    side = width // 2
    numbers = numbers[:, :3, :rows].astype(jnp.int32)
    code_all = numbers[:, 0] + 256 * numbers[:, 1] + 65536 * numbers[:, 2]
    code_all = code_all.reshape(all_rows, 1)
    clean_all = code_all // ratio_table.shape[0]
    level_all = code_all % ratio_table.shape[0]
    level_labels = jnp.arange(ratio_table.shape[0], dtype=jnp.int32)
    ratio_rows = jnp.sum(
        jnp.where(level_all == level_labels[None, :], ratio_table[None, :], 0.0),
        axis=1,
        keepdims=True,
    )
    columns = (e_at * n_vocab + v_at) * tile + jnp.arange(tile, dtype=jnp.int32)
    scores = wide_dot(normed_near, head_turned[:side], ((1,), (0,))) + wide_dot(
        normed_far, head_turned[side:], ((1,), (0,))
    )
    target_hit = (clean_all == columns[None, :]).astype(f32)
    loss_scale = 1.0 / math.sqrt(all_rows)
    score_grad = ((jnp.exp(scores) - ratio_rows * target_hit) * loss_scale).astype(bf16)
    along = jnp.sum(score_grad.astype(f32) * scores, axis=1)
    score_grad, along = lax.optimization_barrier((score_grad, along))
    far = wide_dot(score_grad, head_turned[side:], ((1,), (1,))).astype(bf16)
    far = across_core(far)
    kept, *sent = near_gradient(score_grad, head_turned[:side], far)
    kept, sent, score_grad, along = lax.optimization_barrier((kept, sent, score_grad, along))
    sent = [along_x(a, k + 1) for k, a in enumerate(sent)]
    along = jnp.pad(along.reshape(n_expert, 1, rows), ((0, 0), (0, 7), (0, 128 - rows)))
    along = jnp.sum(exchanged(along, ("y", "z")), axis=0)
    along = along + across_core(along)
    along = along + sum(along_x(along, k) for k in range(1, XN))
    along, score_grad = lax.optimization_barrier((along, score_grad))
    head_grad = head_gradient(order, normed_near, normed_far, score_grad)
    sent, head_grad, along = lax.optimization_barrier((sent, head_grad, along))
    kept = (kept + sum(a.astype(f32) for a in sent)).astype(bf16)
    kept = exchanged(kept.reshape(n_expert, rows, share), ("y", "z"))
    normed_grad = jnp.sum(kept.astype(f32), axis=0)

    residual_grad = (
        gain_share * normed_grad - unit_share * (along[0, :rows] / width)[:, None]
    ) / row_scale

    routed = wide_dot(pick, residual_grad, ((1,), (0,)), lax.Precision.HIGHEST)
    routed = (slot_gate * routed).astype(bf16).reshape(n_expert, own_experts * capacity, share)
    routed = exchanged(routed, ("y", "z"))
    routed, inputs = lax.optimization_barrier((routed, inputs))
    gate_pre = jnp.einsum("esd,edf->esf", inputs, w_gate, preferred_element_type=f32)
    up_pre = jnp.einsum("esd,edf->esf", inputs, w_up, preferred_element_type=f32)
    grads = in_ring_order(by_expert(routed), along_x, XN)
    grads, gate_pre, up_pre = lax.optimization_barrier((grads, gate_pre, up_pre))
    grads = jnp.concatenate(grads, axis=2)
    grads_far = across_core(grads)

    act_grad = jnp.einsum(
        "esd,efd->esf", grads, down_turned[:, :, :side], preferred_element_type=f32
    ) + jnp.einsum(
        "esd,efd->esf", grads_far, down_turned[:, :, side:], preferred_element_type=f32
    )
    sigmoid_gate = jax.nn.sigmoid(gate_pre)
    gate_grad = (
        act_grad * up_pre * sigmoid_gate * (1.0 + gate_pre * (1.0 - sigmoid_gate))
    ).astype(bf16)
    up_grad = (act_grad * gate_pre * sigmoid_gate).astype(bf16)
    pair_grad = jnp.concatenate([gate_grad, up_grad], axis=2)

    far = jnp.einsum("esf,edf->esd", pair_grad, pair_turned[:, side:], preferred_element_type=f32)
    far = across_core(far.astype(bf16))
    near = jnp.einsum("esf,edf->esd", pair_grad, pair_turned[:, :side], preferred_element_type=f32)
    near = near + far.astype(f32)
    near = near[:, :, :share] + sum(
        along_x(near[:, :, k * share:(k + 1) * share].astype(bf16), k).astype(f32)
        for k in range(1, XN)
    )
    near = near.reshape(own_experts, n_expert, capacity, share)
    near = near.transpose(1, 0, 2, 3).reshape(n_expert, own_experts * capacity, share)
    returned = lax.all_to_all(near, ("y", "z"), 0, 0, tiled=True)
    input_grad = wide_dot(
        pick,
        returned.reshape(experts * capacity, share),
        ((0,), (0,)),
        lax.Precision.HIGHEST,
    )
    return (head_grad, residual_grad, input_grad)


def solution(mesh):
    fine = Mesh(mesh.devices.reshape(YN, ZN, XN, CN), ("y", "z", "x", "core"))
    expert, vocab = ("y", "z"), ("x", "core")
    everywhere = expert + vocab
    in_specs = (
        P(expert, None),
        P(expert, None),
        P(),
        P(None, everywhere),
        P(expert),
        P(expert),
        P(),
        P(expert, None),
        P(expert, None),
        P(expert, None, vocab),
        P(expert, None, vocab),
        P(expert, vocab, None),
    )
    out_specs = (P(None, everywhere), P(expert, vocab), P(expert, vocab))
    return jax.shard_map(
        on_device, mesh=fine, in_specs=in_specs, out_specs=out_specs, check_vma=False
    )
```

```python
import math

import jax
import jax.numpy as jnp
from jax import lax
from jax.experimental import pallas as pl
from jax.experimental.pallas import tpu as pltpu
from jax.sharding import Mesh, PartitionSpec as P

epsilon = 1e-05
YN, ZN, XN, CN = 4, 8, 4, 2
bf16 = jnp.bfloat16
f32 = jnp.float32


def wide_dot(a, b, dims, precision=None):
    return lax.dot_general(
        a, b, (dims, ((), ())), preferred_element_type=f32, precision=precision
    )


def along_y(a, step):
    return lax.ppermute(a, "y", [(p, (p + step) % YN) for p in range(YN)])


def along_x(a, step):
    return lax.ppermute(a, "x", [(p, (p + step) % XN) for p in range(XN)])


def across_core(a):
    return lax.ppermute(a, "core", [(p, CN - 1 - p) for p in range(CN)])


def exchanged(a, axes):
    return lax.all_to_all(a, axes, 0, 0, tiled=True)


def in_ring_order(a, move, ring):
    return [a] + [move(a, ring - k) for k in range(1, ring)]


def turned_weights(order, head_weight, w_gate, w_up, w_down):
    width, tile = head_weight.shape
    own, _, hidden = w_gate.shape
    count = order.shape[0]
    share = width // count

    lead = count // 2

    def body(
        order_ref, head_ref, gate_ref, up_ref, down_ref, near_out, far_out, pair_out, down_out
    ):
        @pl.when(pl.program_id(0) < lead)
        def _():
            near_out[...] = head_ref[...]

        @pl.when(pl.program_id(0) >= lead)
        def _():
            far_out[...] = head_ref[...]

        pair_out[:, :, :hidden] = gate_ref[...]
        pair_out[:, :, hidden:] = up_ref[...]
        down_out[...] = down_ref[...]

    moved = 2 * (head_weight.size + 3 * w_gate.size)
    return pl.pallas_call(
        body,
        grid_spec=pltpu.PrefetchScalarGridSpec(
            num_scalar_prefetch=1,
            grid=(count,),
            in_specs=[
                pl.BlockSpec((share, tile), lambda i, s: (s[i], 0)),
                pl.BlockSpec((own, share, hidden), lambda i, s: (0, s[i], 0)),
                pl.BlockSpec((own, share, hidden), lambda i, s: (0, s[i], 0)),
                pl.BlockSpec((own, hidden, share), lambda i, s: (0, 0, s[i])),
            ],
            out_specs=[
                pl.BlockSpec((share, tile), lambda i, s: (jnp.minimum(i, lead - 1), 0)),
                pl.BlockSpec((share, tile), lambda i, s: (jnp.maximum(i - lead, 0), 0)),
                pl.BlockSpec((own, share, 2 * hidden), lambda i, s: (0, i, 0)),
                pl.BlockSpec((own, hidden, share), lambda i, s: (0, 0, i)),
            ],
        ),
        out_shape=[
            jax.ShapeDtypeStruct((width // 2, tile), bf16),
            jax.ShapeDtypeStruct((width // 2, tile), bf16),
            jax.ShapeDtypeStruct((own, width, 2 * hidden), bf16),
            jax.ShapeDtypeStruct((own, hidden, width), bf16),
        ],
        cost_estimate=pl.CostEstimate(flops=0, bytes_accessed=2 * moved, transcendentals=0),
        name="turned_weights",
    )(order, head_weight, w_gate, w_up, w_down)


def head_gradient(order, near, far, score_grad):
    rows, side = near.shape
    tile = score_grad.shape[1]
    count = order.shape[0]
    share = 2 * side // count
    lead = count // 2

    def body(order_ref, near_ref, far_ref, grad_ref, out_ref):
        def product(rows_ref):
            out_ref[...] = wide_dot(rows_ref[...], grad_ref[...], ((0,), (0,)))

        @pl.when(pl.program_id(0) < lead)
        def _():
            product(near_ref)

        @pl.when(pl.program_id(0) >= lead)
        def _():
            product(far_ref)

    return pl.pallas_call(
        body,
        grid_spec=pltpu.PrefetchScalarGridSpec(
            num_scalar_prefetch=1,
            grid=(count,),
            in_specs=[
                pl.BlockSpec((rows, share), lambda i, s: (0, jnp.minimum(i, lead - 1))),
                pl.BlockSpec((rows, share), lambda i, s: (0, jnp.maximum(i - lead, 0))),
                pl.BlockSpec((rows, tile), lambda i, s: (0, 0)),
            ],
            out_specs=pl.BlockSpec((share, tile), lambda i, s: (s[i], 0)),
        ),
        out_shape=jax.ShapeDtypeStruct((2 * side, tile), f32),
        cost_estimate=pl.CostEstimate(flops=1024, bytes_accessed=1024, transcendentals=0),
        name="head_gradient",
    )(order, near, far, score_grad)


def near_gradient(score_grad, weight, far):
    rows, tile = score_grad.shape
    share = weight.shape[0] // XN
    part = rows // YN

    def body(grad_ref, weight_ref, far_ref, *outs):
        for k in range(XN):
            low = slice(k * share, (k + 1) * share)
            for i in range(YN):
                at = slice(i * part, (i + 1) * part)
                total = wide_dot(grad_ref[at, :], weight_ref[low, :], ((1,), (1,)))
                total = total + far_ref[at, low].astype(f32)
                outs[k][at, :] = total.astype(outs[k].dtype)

    whole = pl.BlockSpec(memory_space=pltpu.VMEM)
    return pl.pallas_call(
        body,
        in_specs=[whole] * 3,
        out_specs=[whole] * XN,
        out_shape=[
            jax.ShapeDtypeStruct((rows, share), t) for t in [f32] + [bf16] * (XN - 1)
        ],
        cost_estimate=pl.CostEstimate(
            flops=2 * rows * tile * share * XN,
            bytes_accessed=8 * rows * share * XN,
            transcendentals=0,
        ),
        compiler_params=pltpu.CompilerParams(vmem_limit_bytes=32 * 1024 * 1024),
        name="near_gradient",
    )(score_grad, weight, far)


def on_device(
    layer_out,
    moe_input,
    final_gain,
    head_weight,
    clean_ids,
    levels,
    ratio_table,
    gate_weights,
    expert_ids,
    w_gate,
    w_up,
    w_down,
):
    rows, width = layer_out.shape
    n_expert = YN * ZN
    n_vocab = XN * CN
    all_rows = rows * n_expert
    own_experts = w_gate.shape[0]
    experts = own_experts * n_expert
    capacity = max(2, 2 * rows * expert_ids.shape[1] // experts)
    share = width // n_vocab
    tile = head_weight.shape[1]
    y_at, x_at, c_at = lax.axis_index("y"), lax.axis_index("x"), lax.axis_index("core")
    e_at = y_at * ZN + lax.axis_index("z")
    v_at = x_at * CN + c_at

    order = jnp.stack(
        [((x_at + k) % XN) * CN + (c_at + c) % CN for c in range(CN) for k in range(XN)]
    )
    head_near, head_far, pair_turned, down_turned = turned_weights(
        order, head_weight, w_gate, w_up, w_down
    )

    values = layer_out.astype(f32)
    row_scale = jnp.sqrt(jnp.mean(values * values, axis=1, keepdims=True) + epsilon)
    unit_share = (
        lax.dynamic_slice_in_dim(layer_out, v_at * share, share, 1).astype(f32) / row_scale
    )
    gain_share = lax.dynamic_slice_in_dim(final_gain, v_at * share, share, 0)[None, :]
    normed_share = (unit_share * gain_share).astype(bf16)

    labels = jnp.arange(experts, dtype=jnp.int32)
    hits = expert_ids[:, :, None] == labels
    naming = jnp.sum(hits.astype(f32), axis=1)
    before = (jnp.arange(rows)[:, None] > jnp.arange(rows)[None, :]).astype(f32)
    earlier = wide_dot(before, naming, ((1,), (0,)))
    gates = jnp.sum(jnp.where(hits, gate_weights[:, :, None], 0.0), axis=1)
    slots = jnp.arange(capacity, dtype=f32)
    taken = (earlier.T[:, None, :] == slots[None, :, None]) & (naming.T[:, None, :] > 0)
    slot_gate = jnp.sum(jnp.where(taken, gates.T[:, None, :], 0.0), axis=2)
    pick = taken.astype(f32).reshape(experts * capacity, rows)
    slot_gate = slot_gate.reshape(experts * capacity, 1)

    def by_expert(a):
        a = a.reshape(n_expert, own_experts, capacity, a.shape[-1])
        return a.transpose(1, 0, 2, 3).reshape(own_experts, n_expert * capacity, a.shape[-1])

    moe_share = lax.dynamic_slice_in_dim(moe_input, v_at * share, share, 1)
    inputs = wide_dot(pick.astype(bf16), moe_share, ((1,), (0,))).astype(bf16)
    inputs = inputs.reshape(n_expert, own_experts * capacity, share)

    code = clean_ids * ratio_table.shape[0] + levels
    digits = jnp.stack([code % 256, code // 256 % 256, code // 65536]).astype(bf16)
    digits = jnp.pad(digits, ((0, 8 - digits.shape[0]), (0, share - rows)))
    spread = jnp.broadcast_to(
        jnp.concatenate([normed_share, digits], axis=0)[None], (n_expert, rows + 8, share)
    )
    spread = exchanged(spread, ("y", "z"))
    spread, head_near, head_far, pair_turned, down_turned, inputs, pick, slot_gate = (
        lax.optimization_barrier(
            (spread, head_near, head_far, pair_turned, down_turned, inputs, pick, slot_gate)
        )
    )
    numbers = spread[:, rows:]
    normed_near = in_ring_order(spread[:, :rows].reshape(all_rows, share), along_x, XN)
    inputs = exchanged(inputs, ("y", "z"))
    normed_near, inputs = lax.optimization_barrier((normed_near, inputs))
    normed_near = jnp.concatenate(normed_near, axis=1)
    normed_far = across_core(normed_near)

    inputs = lax.all_gather(by_expert(inputs), ("x", "core"), axis=2, tiled=True)

    side = width // 2
    numbers = numbers[:, :3, :rows].astype(jnp.int32)
    code_all = numbers[:, 0] + 256 * numbers[:, 1] + 65536 * numbers[:, 2]
    code_all = code_all.reshape(all_rows, 1)
    clean_all = code_all // ratio_table.shape[0]
    level_all = code_all % ratio_table.shape[0]
    level_labels = jnp.arange(ratio_table.shape[0], dtype=jnp.int32)
    ratio_rows = jnp.sum(
        jnp.where(level_all == level_labels[None, :], ratio_table[None, :], 0.0),
        axis=1,
        keepdims=True,
    )
    columns = (e_at * n_vocab + v_at) * tile + jnp.arange(tile, dtype=jnp.int32)
    scores = wide_dot(normed_near, head_near, ((1,), (0,)))
    scores, normed_far = lax.optimization_barrier((scores, normed_far))
    scores = scores + wide_dot(normed_far, head_far, ((1,), (0,)))
    target_hit = (clean_all == columns[None, :]).astype(f32)
    loss_scale = 1.0 / math.sqrt(all_rows)
    score_grad = ((jnp.exp(scores) - ratio_rows * target_hit) * loss_scale).astype(bf16)
    along = jnp.sum(score_grad.astype(f32) * scores, axis=1)
    score_grad, along = lax.optimization_barrier((score_grad, along))
    far = wide_dot(score_grad, head_far, ((1,), (1,))).astype(bf16)
    far = across_core(far)
    along = along.reshape(8, all_rows // 8)
    along = along + across_core(along)
    along = along + sum(along_x(along, k) for k in range(1, XN))
    along, far = lax.optimization_barrier((along, far))
    kept, *sent = near_gradient(score_grad, head_near, far)
    kept, sent, score_grad, along = lax.optimization_barrier((kept, sent, score_grad, along))
    sent = [along_x(a, k + 1) for k, a in enumerate(sent)]
    along = jnp.pad(along.reshape(n_expert, 1, rows), ((0, 0), (0, 7), (0, 128 - rows)))
    along = jnp.sum(exchanged(along, ("y", "z")), axis=0)
    head_grad = head_gradient(order, normed_near, normed_far, score_grad)
    sent, head_grad, along = lax.optimization_barrier((sent, head_grad, along))
    kept = (kept + sum(a.astype(f32) for a in sent)).astype(bf16)
    kept = exchanged(kept.reshape(n_expert, rows, share), ("y", "z"))
    normed_grad = jnp.sum(kept.astype(f32), axis=0)

    residual_grad = (
        gain_share * normed_grad - unit_share * (along[0, :rows] / width)[:, None]
    ) / row_scale

    routed = wide_dot(pick, residual_grad, ((1,), (0,)), lax.Precision.HIGHEST)
    routed = (slot_gate * routed).astype(bf16).reshape(n_expert, own_experts * capacity, share)
    routed = exchanged(routed, ("y", "z"))
    routed, inputs = lax.optimization_barrier((routed, inputs))
    gate_pre = jnp.einsum("esd,edf->esf", inputs, w_gate, preferred_element_type=f32)
    up_pre = jnp.einsum("esd,edf->esf", inputs, w_up, preferred_element_type=f32)
    grads = in_ring_order(by_expert(routed), along_x, XN)
    grads, gate_pre, up_pre = lax.optimization_barrier((grads, gate_pre, up_pre))
    grads = jnp.concatenate(grads, axis=2)
    grads_far = across_core(grads)

    act_grad = jnp.einsum(
        "esd,efd->esf", grads, down_turned[:, :, :side], preferred_element_type=f32
    ) + jnp.einsum(
        "esd,efd->esf", grads_far, down_turned[:, :, side:], preferred_element_type=f32
    )
    sigmoid_gate = jax.nn.sigmoid(gate_pre)
    gate_grad = (
        act_grad * up_pre * sigmoid_gate * (1.0 + gate_pre * (1.0 - sigmoid_gate))
    ).astype(bf16)
    up_grad = (act_grad * gate_pre * sigmoid_gate).astype(bf16)
    pair_grad = jnp.concatenate([gate_grad, up_grad], axis=2)

    far = jnp.einsum("esf,edf->esd", pair_grad, pair_turned[:, side:], preferred_element_type=f32)
    far = across_core(far.astype(bf16))
    near = jnp.einsum("esf,edf->esd", pair_grad, pair_turned[:, :side], preferred_element_type=f32)
    near = near + far.astype(f32)
    near = near[:, :, :share] + sum(
        along_x(near[:, :, k * share:(k + 1) * share].astype(bf16), k).astype(f32)
        for k in range(1, XN)
    )
    near = near.reshape(own_experts, n_expert, capacity, share)
    near = near.transpose(1, 0, 2, 3).reshape(n_expert, own_experts * capacity, share)
    returned = lax.all_to_all(near, ("y", "z"), 0, 0, tiled=True)
    input_grad = wide_dot(
        pick,
        returned.reshape(experts * capacity, share),
        ((0,), (0,)),
        lax.Precision.HIGHEST,
    )
    return (head_grad, residual_grad, input_grad)


def solution(mesh):
    fine = Mesh(mesh.devices.reshape(YN, ZN, XN, CN), ("y", "z", "x", "core"))
    expert, vocab = ("y", "z"), ("x", "core")
    everywhere = expert + vocab
    in_specs = (
        P(expert, None),
        P(expert, None),
        P(),
        P(None, everywhere),
        P(expert),
        P(expert),
        P(),
        P(expert, None),
        P(expert, None),
        P(expert, None, vocab),
        P(expert, None, vocab),
        P(expert, vocab, None),
    )
    out_specs = (P(None, everywhere), P(expert, vocab), P(expert, vocab))
    return jax.shard_map(
        on_device, mesh=fine, in_specs=in_specs, out_specs=out_specs, check_vma=False
    )
```

```python
import math

import jax
import jax.numpy as jnp
from jax import lax
from jax.experimental import pallas as pl
from jax.experimental.pallas import tpu as pltpu
from jax.sharding import Mesh, PartitionSpec as P

epsilon = 1e-05
YN, ZN, XN, CN = 4, 8, 4, 2
bf16 = jnp.bfloat16
f32 = jnp.float32


def wide_dot(a, b, dims, precision=None):
    return lax.dot_general(
        a, b, (dims, ((), ())), preferred_element_type=f32, precision=precision
    )


def along_y(a, step):
    return lax.ppermute(a, "y", [(p, (p + step) % YN) for p in range(YN)])


def along_x(a, step):
    return lax.ppermute(a, "x", [(p, (p + step) % XN) for p in range(XN)])


def across_core(a):
    return lax.ppermute(a, "core", [(p, CN - 1 - p) for p in range(CN)])


def exchanged(a, axes):
    return lax.all_to_all(a, axes, 0, 0, tiled=True)


def in_ring_order(a, move, ring):
    return [a] + [move(a, ring - k) for k in range(1, ring)]


def normed_to_spread(at, layer_out, final_gain, digits, copies):
    rows, width = layer_out.shape
    below, share = digits.shape

    def body(at_ref, rows_ref, gain_ref, digits_ref, spread_out, unit_out, scale_out, gain_out):
        low = pl.multiple_of(at_ref[0] * share, share)
        values = rows_ref[...].astype(f32)
        mean = jnp.sum(values * values, axis=1, keepdims=True) / width
        scale = jnp.sqrt(mean + epsilon)
        unit = rows_ref[:, pl.ds(low, share)].astype(f32) / scale
        gain = gain_ref[:, pl.ds(low, share)]
        normed = (unit * gain).astype(bf16)
        for k in range(copies):
            spread_out[k, :rows, :] = normed
            spread_out[k, rows:, :] = digits_ref[...]
        unit_out[...] = unit
        scale_out[...] = scale
        gain_out[...] = gain

    whole = pl.BlockSpec(memory_space=pltpu.VMEM)
    return pl.pallas_call(
        body,
        in_specs=[pl.BlockSpec(memory_space=pltpu.SMEM)] + [whole] * 3,
        out_specs=[whole] * 4,
        out_shape=[
            jax.ShapeDtypeStruct((copies, rows + below, share), bf16),
            jax.ShapeDtypeStruct((rows, share), f32),
            jax.ShapeDtypeStruct((rows, 1), f32),
            jax.ShapeDtypeStruct((1, share), f32),
        ],
        name="normed_to_spread",
    )(at[None], layer_out, final_gain[None, :], digits)


def turned_weights(order, head_weight, w_gate, w_up, w_down):
    width, tile = head_weight.shape
    own, _, hidden = w_gate.shape
    count = order.shape[0]
    share = width // count

    lead = count // 2

    def body(
        order_ref, head_ref, gate_ref, up_ref, down_ref, near_out, far_out, pair_out, down_out
    ):
        @pl.when(pl.program_id(0) < lead)
        def _():
            near_out[...] = head_ref[...]

        @pl.when(pl.program_id(0) >= lead)
        def _():
            far_out[...] = head_ref[...]

        pair_out[:, :, :hidden] = gate_ref[...]
        pair_out[:, :, hidden:] = up_ref[...]
        down_out[...] = down_ref[...]

    moved = 2 * (head_weight.size + 3 * w_gate.size)
    return pl.pallas_call(
        body,
        grid_spec=pltpu.PrefetchScalarGridSpec(
            num_scalar_prefetch=1,
            grid=(count,),
            in_specs=[
                pl.BlockSpec((share, tile), lambda i, s: (s[i], 0)),
                pl.BlockSpec((own, share, hidden), lambda i, s: (0, s[i], 0)),
                pl.BlockSpec((own, share, hidden), lambda i, s: (0, s[i], 0)),
                pl.BlockSpec((own, hidden, share), lambda i, s: (0, 0, s[i])),
            ],
            out_specs=[
                pl.BlockSpec((share, tile), lambda i, s: (jnp.minimum(i, lead - 1), 0)),
                pl.BlockSpec((share, tile), lambda i, s: (jnp.maximum(i - lead, 0), 0)),
                pl.BlockSpec((own, share, 2 * hidden), lambda i, s: (0, i, 0)),
                pl.BlockSpec((own, hidden, share), lambda i, s: (0, 0, i)),
            ],
        ),
        out_shape=[
            jax.ShapeDtypeStruct((width // 2, tile), bf16),
            jax.ShapeDtypeStruct((width // 2, tile), bf16),
            jax.ShapeDtypeStruct((own, width, 2 * hidden), bf16),
            jax.ShapeDtypeStruct((own, hidden, width), bf16),
        ],
        cost_estimate=pl.CostEstimate(flops=0, bytes_accessed=2 * moved, transcendentals=0),
        name="turned_weights",
    )(order, head_weight, w_gate, w_up, w_down)


def head_gradient(order, near, far, score_grad):
    rows, side = near.shape
    tile = score_grad.shape[1]
    count = order.shape[0]
    share = 2 * side // count
    lead = count // 2

    def body(order_ref, near_ref, far_ref, grad_ref, out_ref):
        def product(rows_ref):
            out_ref[...] = wide_dot(rows_ref[...], grad_ref[...], ((0,), (0,)))

        @pl.when(pl.program_id(0) < lead)
        def _():
            product(near_ref)

        @pl.when(pl.program_id(0) >= lead)
        def _():
            product(far_ref)

    return pl.pallas_call(
        body,
        grid_spec=pltpu.PrefetchScalarGridSpec(
            num_scalar_prefetch=1,
            grid=(count,),
            in_specs=[
                pl.BlockSpec((rows, share), lambda i, s: (0, jnp.minimum(i, lead - 1))),
                pl.BlockSpec((rows, share), lambda i, s: (0, jnp.maximum(i - lead, 0))),
                pl.BlockSpec((rows, tile), lambda i, s: (0, 0)),
            ],
            out_specs=pl.BlockSpec((share, tile), lambda i, s: (s[i], 0)),
        ),
        out_shape=jax.ShapeDtypeStruct((2 * side, tile), f32),
        cost_estimate=pl.CostEstimate(flops=1024, bytes_accessed=1024, transcendentals=0),
        name="head_gradient",
    )(order, near, far, score_grad)


def near_gradient(score_grad, weight, far):
    rows, tile = score_grad.shape
    share = weight.shape[0] // XN
    part = rows // YN

    def body(grad_ref, weight_ref, far_ref, *outs):
        for k in range(XN):
            low = slice(k * share, (k + 1) * share)
            for i in range(YN):
                at = slice(i * part, (i + 1) * part)
                total = wide_dot(grad_ref[at, :], weight_ref[low, :], ((1,), (1,)))
                total = total + far_ref[at, low].astype(f32)
                outs[k][at, :] = total.astype(outs[k].dtype)

    whole = pl.BlockSpec(memory_space=pltpu.VMEM)
    return pl.pallas_call(
        body,
        in_specs=[whole] * 3,
        out_specs=[whole] * XN,
        out_shape=[
            jax.ShapeDtypeStruct((rows, share), t) for t in [f32] + [bf16] * (XN - 1)
        ],
        cost_estimate=pl.CostEstimate(
            flops=2 * rows * tile * share * XN,
            bytes_accessed=8 * rows * share * XN,
            transcendentals=0,
        ),
        compiler_params=pltpu.CompilerParams(vmem_limit_bytes=32 * 1024 * 1024),
        name="near_gradient",
    )(score_grad, weight, far)


def on_device(
    layer_out,
    moe_input,
    final_gain,
    head_weight,
    clean_ids,
    levels,
    ratio_table,
    gate_weights,
    expert_ids,
    w_gate,
    w_up,
    w_down,
):
    rows, width = layer_out.shape
    n_expert = YN * ZN
    n_vocab = XN * CN
    all_rows = rows * n_expert
    own_experts = w_gate.shape[0]
    experts = own_experts * n_expert
    capacity = max(2, 2 * rows * expert_ids.shape[1] // experts)
    share = width // n_vocab
    tile = head_weight.shape[1]
    y_at, x_at, c_at = lax.axis_index("y"), lax.axis_index("x"), lax.axis_index("core")
    e_at = y_at * ZN + lax.axis_index("z")
    v_at = x_at * CN + c_at

    order = jnp.stack(
        [((x_at + k) % XN) * CN + (c_at + c) % CN for c in range(CN) for k in range(XN)]
    )
    head_near, head_far, pair_turned, down_turned = turned_weights(
        order, head_weight, w_gate, w_up, w_down
    )

    code = clean_ids * ratio_table.shape[0] + levels
    digits = jnp.stack([code % 256, code // 256 % 256, code // 65536]).astype(bf16)
    digits = jnp.pad(digits, ((0, 8 - digits.shape[0]), (0, share - rows)))
    spread, unit_share, row_scale, gain_share = normed_to_spread(
        v_at, layer_out, final_gain, digits, n_expert
    )

    labels = jnp.arange(experts, dtype=jnp.int32)
    hits = expert_ids[:, :, None] == labels
    naming = jnp.sum(hits.astype(f32), axis=1)
    before = (jnp.arange(rows)[:, None] > jnp.arange(rows)[None, :]).astype(f32)
    earlier = wide_dot(before, naming, ((1,), (0,)))
    gates = jnp.sum(jnp.where(hits, gate_weights[:, :, None], 0.0), axis=1)
    slots = jnp.arange(capacity, dtype=f32)
    taken = (earlier.T[:, None, :] == slots[None, :, None]) & (naming.T[:, None, :] > 0)
    slot_gate = jnp.sum(jnp.where(taken, gates.T[:, None, :], 0.0), axis=2)
    pick = taken.astype(f32).reshape(experts * capacity, rows)
    slot_gate = slot_gate.reshape(experts * capacity, 1)

    def by_expert(a):
        a = a.reshape(n_expert, own_experts, capacity, a.shape[-1])
        return a.transpose(1, 0, 2, 3).reshape(own_experts, n_expert * capacity, a.shape[-1])

    moe_share = lax.dynamic_slice_in_dim(moe_input, v_at * share, share, 1)
    inputs = wide_dot(pick.astype(bf16), moe_share, ((1,), (0,))).astype(bf16)
    inputs = inputs.reshape(n_expert, own_experts * capacity, share)

    spread = exchanged(spread, ("y", "z"))
    spread, head_near, head_far, pair_turned, down_turned, inputs, pick, slot_gate = (
        lax.optimization_barrier(
            (spread, head_near, head_far, pair_turned, down_turned, inputs, pick, slot_gate)
        )
    )
    numbers = spread[:, rows:]
    normed_near = in_ring_order(spread[:, :rows].reshape(all_rows, share), along_x, XN)
    inputs = exchanged(inputs, ("y", "z"))
    normed_near, inputs = lax.optimization_barrier((normed_near, inputs))
    normed_near = jnp.concatenate(normed_near, axis=1)
    normed_far = across_core(normed_near)

    inputs = lax.all_gather(by_expert(inputs), ("x", "core"), axis=2, tiled=True)

    side = width // 2
    numbers = numbers[:, :3, :rows].astype(jnp.int32)
    code_all = numbers[:, 0] + 256 * numbers[:, 1] + 65536 * numbers[:, 2]
    code_all = code_all.reshape(all_rows, 1)
    clean_all = code_all // ratio_table.shape[0]
    level_all = code_all % ratio_table.shape[0]
    level_labels = jnp.arange(ratio_table.shape[0], dtype=jnp.int32)
    ratio_rows = jnp.sum(
        jnp.where(level_all == level_labels[None, :], ratio_table[None, :], 0.0),
        axis=1,
        keepdims=True,
    )
    columns = (e_at * n_vocab + v_at) * tile + jnp.arange(tile, dtype=jnp.int32)
    scores = wide_dot(normed_near, head_near, ((1,), (0,)))
    scores, normed_far = lax.optimization_barrier((scores, normed_far))
    scores = scores + wide_dot(normed_far, head_far, ((1,), (0,)))
    target_hit = (clean_all == columns[None, :]).astype(f32)
    loss_scale = 1.0 / math.sqrt(all_rows)
    score_grad = ((jnp.exp(scores) - ratio_rows * target_hit) * loss_scale).astype(bf16)
    along = jnp.sum(score_grad.astype(f32) * scores, axis=1)
    score_grad, along = lax.optimization_barrier((score_grad, along))
    far = wide_dot(score_grad, head_far, ((1,), (1,))).astype(bf16)
    far = across_core(far)
    kept, *sent = near_gradient(score_grad, head_near, far)
    kept, sent, score_grad, along = lax.optimization_barrier((kept, sent, score_grad, along))
    sent = [along_x(a, k + 1) for k, a in enumerate(sent)]
    along = jnp.pad(along.reshape(n_expert, 1, rows), ((0, 0), (0, 7), (0, 128 - rows)))
    along = jnp.sum(exchanged(along, ("y", "z")), axis=0)
    head_grad = head_gradient(order, normed_near, normed_far, score_grad)
    sent, head_grad, along = lax.optimization_barrier((sent, head_grad, along))
    along = along + across_core(along)
    along = along + sum(along_x(along, k) for k in range(1, XN))
    kept = (kept + sum(a.astype(f32) for a in sent)).astype(bf16)
    kept = exchanged(kept.reshape(n_expert, rows, share), ("y", "z"))
    normed_grad = jnp.sum(kept.astype(f32), axis=0)

    residual_grad = (
        gain_share * normed_grad - unit_share * (along[0, :rows] / width)[:, None]
    ) / row_scale

    routed = wide_dot(pick, residual_grad, ((1,), (0,)), lax.Precision.HIGHEST)
    routed = (slot_gate * routed).astype(bf16).reshape(n_expert, own_experts * capacity, share)
    routed = exchanged(routed, ("y", "z"))
    routed, inputs = lax.optimization_barrier((routed, inputs))
    gate_pre = jnp.einsum("esd,edf->esf", inputs, w_gate, preferred_element_type=f32)
    up_pre = jnp.einsum("esd,edf->esf", inputs, w_up, preferred_element_type=f32)
    grads = in_ring_order(by_expert(routed), along_x, XN)
    grads, gate_pre, up_pre = lax.optimization_barrier((grads, gate_pre, up_pre))
    grads = jnp.concatenate(grads, axis=2)
    grads_far = across_core(grads)

    act_grad = jnp.einsum(
        "esd,efd->esf", grads, down_turned[:, :, :side], preferred_element_type=f32
    ) + jnp.einsum(
        "esd,efd->esf", grads_far, down_turned[:, :, side:], preferred_element_type=f32
    )
    sigmoid_gate = jax.nn.sigmoid(gate_pre)
    gate_grad = (
        act_grad * up_pre * sigmoid_gate * (1.0 + gate_pre * (1.0 - sigmoid_gate))
    ).astype(bf16)
    up_grad = (act_grad * gate_pre * sigmoid_gate).astype(bf16)
    pair_grad = jnp.concatenate([gate_grad, up_grad], axis=2)

    far = jnp.einsum("esf,edf->esd", pair_grad, pair_turned[:, side:], preferred_element_type=f32)
    far = across_core(far.astype(bf16))
    near = jnp.einsum("esf,edf->esd", pair_grad, pair_turned[:, :side], preferred_element_type=f32)
    near = near + far.astype(f32)
    near = near[:, :, :share] + sum(
        along_x(near[:, :, k * share:(k + 1) * share].astype(bf16), k).astype(f32)
        for k in range(1, XN)
    )
    near = near.reshape(own_experts, n_expert, capacity, share)
    near = near.transpose(1, 0, 2, 3).reshape(n_expert, own_experts * capacity, share)
    returned = lax.all_to_all(near, ("y", "z"), 0, 0, tiled=True)
    input_grad = wide_dot(
        pick,
        returned.reshape(experts * capacity, share),
        ((0,), (0,)),
        lax.Precision.HIGHEST,
    )
    return (head_grad, residual_grad, input_grad)


def solution(mesh):
    fine = Mesh(mesh.devices.reshape(YN, ZN, XN, CN), ("y", "z", "x", "core"))
    expert, vocab = ("y", "z"), ("x", "core")
    everywhere = expert + vocab
    in_specs = (
        P(expert, None),
        P(expert, None),
        P(),
        P(None, everywhere),
        P(expert),
        P(expert),
        P(),
        P(expert, None),
        P(expert, None),
        P(expert, None, vocab),
        P(expert, None, vocab),
        P(expert, vocab, None),
    )
    out_specs = (P(None, everywhere), P(expert, vocab), P(expert, vocab))
    return jax.shard_map(
        on_device, mesh=fine, in_specs=in_specs, out_specs=out_specs, check_vma=False
    )
```

```python
import math

import jax
import jax.numpy as jnp
from jax import lax
from jax.experimental import pallas as pl
from jax.experimental.pallas import tpu as pltpu
from jax.sharding import Mesh, PartitionSpec as P

epsilon = 1e-05
YN, ZN, XN, CN = 4, 8, 4, 2
bf16 = jnp.bfloat16
f32 = jnp.float32


def wide_dot(a, b, dims, precision=None):
    return lax.dot_general(
        a, b, (dims, ((), ())), preferred_element_type=f32, precision=precision
    )


def along_y(a, step):
    return lax.ppermute(a, "y", [(p, (p + step) % YN) for p in range(YN)])


def along_x(a, step):
    return lax.ppermute(a, "x", [(p, (p + step) % XN) for p in range(XN)])


def across_core(a):
    return lax.ppermute(a, "core", [(p, CN - 1 - p) for p in range(CN)])


def exchanged(a, axes):
    return lax.all_to_all(a, axes, 0, 0, tiled=True)


def in_ring_order(a, move, ring):
    return [a] + [move(a, ring - k) for k in range(1, ring)]


def normed_to_spread(at, layer_out, final_gain, digits, copies):
    rows, width = layer_out.shape
    below, share = digits.shape

    def body(at_ref, rows_ref, gain_ref, digits_ref, spread_out, unit_out, scale_out, gain_out):
        low = pl.multiple_of(at_ref[0] * share, share)
        values = rows_ref[...].astype(f32)
        mean = jnp.sum(values * values, axis=1, keepdims=True) / width
        scale = jnp.sqrt(mean + epsilon)
        unit = rows_ref[:, pl.ds(low, share)].astype(f32) / scale
        gain = gain_ref[:, pl.ds(low, share)]
        normed = (unit * gain).astype(bf16)
        for k in range(copies):
            spread_out[k, :rows, :] = normed
            spread_out[k, rows:, :] = digits_ref[...]
        unit_out[...] = unit
        scale_out[...] = scale
        gain_out[...] = gain

    whole = pl.BlockSpec(memory_space=pltpu.VMEM)
    return pl.pallas_call(
        body,
        in_specs=[pl.BlockSpec(memory_space=pltpu.SMEM)] + [whole] * 3,
        out_specs=[whole] * 4,
        out_shape=[
            jax.ShapeDtypeStruct((copies, rows + below, share), bf16),
            jax.ShapeDtypeStruct((rows, share), f32),
            jax.ShapeDtypeStruct((rows, 1), f32),
            jax.ShapeDtypeStruct((1, share), f32),
        ],
        name="normed_to_spread",
    )(at[None], layer_out, final_gain[None, :], digits)


def turned_weights(order, head_weight, w_gate, w_up, w_down):
    width, tile = head_weight.shape
    own, _, hidden = w_gate.shape
    count = order.shape[0]
    share = width // count

    lead = count // 2

    def body(
        order_ref, head_ref, gate_ref, up_ref, down_ref, near_out, far_out, pair_out, down_out
    ):
        @pl.when(pl.program_id(0) < lead)
        def _():
            near_out[...] = head_ref[...]

        @pl.when(pl.program_id(0) >= lead)
        def _():
            far_out[...] = head_ref[...]

        pair_out[:, :, :hidden] = gate_ref[...]
        pair_out[:, :, hidden:] = up_ref[...]
        down_out[...] = down_ref[...]

    moved = 2 * (head_weight.size + 3 * w_gate.size)
    return pl.pallas_call(
        body,
        grid_spec=pltpu.PrefetchScalarGridSpec(
            num_scalar_prefetch=1,
            grid=(count,),
            in_specs=[
                pl.BlockSpec((share, tile), lambda i, s: (s[i], 0)),
                pl.BlockSpec((own, share, hidden), lambda i, s: (0, s[i], 0)),
                pl.BlockSpec((own, share, hidden), lambda i, s: (0, s[i], 0)),
                pl.BlockSpec((own, hidden, share), lambda i, s: (0, 0, s[i])),
            ],
            out_specs=[
                pl.BlockSpec((share, tile), lambda i, s: (jnp.minimum(i, lead - 1), 0)),
                pl.BlockSpec((share, tile), lambda i, s: (jnp.maximum(i - lead, 0), 0)),
                pl.BlockSpec((own, share, 2 * hidden), lambda i, s: (0, i, 0)),
                pl.BlockSpec((own, hidden, share), lambda i, s: (0, 0, i)),
            ],
        ),
        out_shape=[
            jax.ShapeDtypeStruct((width // 2, tile), bf16),
            jax.ShapeDtypeStruct((width // 2, tile), bf16),
            jax.ShapeDtypeStruct((own, width, 2 * hidden), bf16),
            jax.ShapeDtypeStruct((own, hidden, width), bf16),
        ],
        cost_estimate=pl.CostEstimate(flops=0, bytes_accessed=2 * moved, transcendentals=0),
        name="turned_weights",
    )(order, head_weight, w_gate, w_up, w_down)


def head_gradient(order, near, far, score_grad):
    rows, side = near.shape
    tile = score_grad.shape[1]
    count = order.shape[0]
    share = 2 * side // count
    lead = count // 2

    def body(order_ref, near_ref, far_ref, grad_ref, out_ref):
        def product(rows_ref):
            out_ref[...] = wide_dot(rows_ref[...], grad_ref[...], ((0,), (0,)))

        @pl.when(pl.program_id(0) < lead)
        def _():
            product(near_ref)

        @pl.when(pl.program_id(0) >= lead)
        def _():
            product(far_ref)

    return pl.pallas_call(
        body,
        grid_spec=pltpu.PrefetchScalarGridSpec(
            num_scalar_prefetch=1,
            grid=(count,),
            in_specs=[
                pl.BlockSpec((rows, share), lambda i, s: (0, jnp.minimum(i, lead - 1))),
                pl.BlockSpec((rows, share), lambda i, s: (0, jnp.maximum(i - lead, 0))),
                pl.BlockSpec((rows, tile), lambda i, s: (0, 0)),
            ],
            out_specs=pl.BlockSpec((share, tile), lambda i, s: (s[i], 0)),
        ),
        out_shape=jax.ShapeDtypeStruct((2 * side, tile), f32),
        cost_estimate=pl.CostEstimate(flops=1024, bytes_accessed=1024, transcendentals=0),
        name="head_gradient",
    )(order, near, far, score_grad)


def near_gradient(score_grad, weight, far):
    rows, tile = score_grad.shape
    share = weight.shape[0] // XN
    part = rows // YN

    def body(grad_ref, weight_ref, far_ref, *outs):
        for k in range(XN):
            low = slice(k * share, (k + 1) * share)
            for i in range(YN):
                at = slice(i * part, (i + 1) * part)
                total = wide_dot(grad_ref[at, :], weight_ref[low, :], ((1,), (1,)))
                total = total + far_ref[at, low].astype(f32)
                outs[k][at, :] = total.astype(outs[k].dtype)

    whole = pl.BlockSpec(memory_space=pltpu.VMEM)
    return pl.pallas_call(
        body,
        in_specs=[whole] * 3,
        out_specs=[whole] * XN,
        out_shape=[
            jax.ShapeDtypeStruct((rows, share), t) for t in [f32] + [bf16] * (XN - 1)
        ],
        cost_estimate=pl.CostEstimate(
            flops=2 * rows * tile * share * XN,
            bytes_accessed=8 * rows * share * XN,
            transcendentals=0,
        ),
        compiler_params=pltpu.CompilerParams(vmem_limit_bytes=16 * 1024 * 1024),
        name="near_gradient",
    )(score_grad, weight, far)


def on_device(
    layer_out,
    moe_input,
    final_gain,
    head_weight,
    clean_ids,
    levels,
    ratio_table,
    gate_weights,
    expert_ids,
    w_gate,
    w_up,
    w_down,
):
    rows, width = layer_out.shape
    n_expert = YN * ZN
    n_vocab = XN * CN
    all_rows = rows * n_expert
    own_experts = w_gate.shape[0]
    experts = own_experts * n_expert
    capacity = max(2, 2 * rows * expert_ids.shape[1] // experts)
    share = width // n_vocab
    tile = head_weight.shape[1]
    y_at, x_at, c_at = lax.axis_index("y"), lax.axis_index("x"), lax.axis_index("core")
    e_at = y_at * ZN + lax.axis_index("z")
    v_at = x_at * CN + c_at

    order = jnp.stack(
        [((x_at + k) % XN) * CN + (c_at + c) % CN for c in range(CN) for k in range(XN)]
    )
    head_near, head_far, pair_turned, down_turned = turned_weights(
        order, head_weight, w_gate, w_up, w_down
    )

    code = clean_ids * ratio_table.shape[0] + levels
    digits = jnp.stack([code % 256, code // 256 % 256, code // 65536]).astype(bf16)
    digits = jnp.pad(digits, ((0, 8 - digits.shape[0]), (0, share - rows)))
    spread, unit_share, row_scale, gain_share = normed_to_spread(
        v_at, layer_out, final_gain, digits, n_expert
    )

    labels = jnp.arange(experts, dtype=jnp.int32)
    hits = expert_ids[:, :, None] == labels
    naming = jnp.sum(hits.astype(f32), axis=1)
    before = (jnp.arange(rows)[:, None] > jnp.arange(rows)[None, :]).astype(f32)
    earlier = wide_dot(before, naming, ((1,), (0,)))
    gates = jnp.sum(jnp.where(hits, gate_weights[:, :, None], 0.0), axis=1)
    slots = jnp.arange(capacity, dtype=f32)
    taken = (earlier.T[:, None, :] == slots[None, :, None]) & (naming.T[:, None, :] > 0)
    slot_gate = jnp.sum(jnp.where(taken, gates.T[:, None, :], 0.0), axis=2)
    pick = taken.astype(f32).reshape(experts * capacity, rows)
    slot_gate = slot_gate.reshape(experts * capacity, 1)

    def by_expert(a):
        a = a.reshape(n_expert, own_experts, capacity, a.shape[-1])
        return a.transpose(1, 0, 2, 3).reshape(own_experts, n_expert * capacity, a.shape[-1])

    moe_share = lax.dynamic_slice_in_dim(moe_input, v_at * share, share, 1)
    inputs = wide_dot(pick.astype(bf16), moe_share, ((1,), (0,))).astype(bf16)
    inputs = inputs.reshape(n_expert, own_experts * capacity, share)

    spread = exchanged(spread, ("y", "z"))
    spread, head_near, head_far, pair_turned, down_turned, inputs, pick, slot_gate = (
        lax.optimization_barrier(
            (spread, head_near, head_far, pair_turned, down_turned, inputs, pick, slot_gate)
        )
    )
    numbers = spread[:, rows:]
    normed_near = in_ring_order(spread[:, :rows].reshape(all_rows, share), along_x, XN)
    inputs = exchanged(inputs, ("y", "z"))
    normed_near, inputs = lax.optimization_barrier((normed_near, inputs))
    normed_near = jnp.concatenate(normed_near, axis=1)
    normed_far = across_core(normed_near)

    side = width // 2
    numbers = numbers[:, :3, :rows].astype(jnp.int32)
    code_all = numbers[:, 0] + 256 * numbers[:, 1] + 65536 * numbers[:, 2]
    code_all = code_all.reshape(all_rows, 1)
    clean_all = code_all // ratio_table.shape[0]
    level_all = code_all % ratio_table.shape[0]
    level_labels = jnp.arange(ratio_table.shape[0], dtype=jnp.int32)
    ratio_rows = jnp.sum(
        jnp.where(level_all == level_labels[None, :], ratio_table[None, :], 0.0),
        axis=1,
        keepdims=True,
    )
    columns = (e_at * n_vocab + v_at) * tile + jnp.arange(tile, dtype=jnp.int32)
    scores = wide_dot(normed_near, head_near, ((1,), (0,)))
    scores, normed_far = lax.optimization_barrier((scores, normed_far))
    scores = scores + wide_dot(normed_far, head_far, ((1,), (0,)))
    target_hit = (clean_all == columns[None, :]).astype(f32)
    loss_scale = 1.0 / math.sqrt(all_rows)
    score_grad = ((jnp.exp(scores) - ratio_rows * target_hit) * loss_scale).astype(bf16)
    along = jnp.sum(score_grad.astype(f32) * scores, axis=1)
    score_grad, along = lax.optimization_barrier((score_grad, along))
    far = wide_dot(score_grad, head_far, ((1,), (1,))).astype(bf16)
    far = across_core(far)
    kept, *sent = near_gradient(score_grad, head_near, far)
    kept, sent, score_grad, along = lax.optimization_barrier((kept, sent, score_grad, along))
    sent = [along_x(a, k + 1) for k, a in enumerate(sent)]
    along = jnp.pad(along.reshape(n_expert, 1, rows), ((0, 0), (0, 7), (0, 128 - rows)))
    along = jnp.sum(exchanged(along, ("y", "z")), axis=0)
    head_grad = head_gradient(order, normed_near, normed_far, score_grad)
    inputs = by_expert(inputs)
    sent, head_grad, along, inputs = lax.optimization_barrier((sent, head_grad, along, inputs))
    inputs = lax.all_gather(inputs, ("x", "core"), axis=2, tiled=True)
    along = along + across_core(along)
    along = along + sum(along_x(along, k) for k in range(1, XN))
    kept = (kept + sum(a.astype(f32) for a in sent)).astype(bf16)
    kept = exchanged(kept.reshape(n_expert, rows, share), ("y", "z"))
    normed_grad = jnp.sum(kept.astype(f32), axis=0)

    residual_grad = (
        gain_share * normed_grad - unit_share * (along[0, :rows] / width)[:, None]
    ) / row_scale

    routed = wide_dot(pick, residual_grad, ((1,), (0,)), lax.Precision.HIGHEST)
    routed = (slot_gate * routed).astype(bf16).reshape(n_expert, own_experts * capacity, share)
    routed = exchanged(routed, ("y", "z"))
    gate_pre = jnp.einsum("esd,edf->esf", inputs, w_gate, preferred_element_type=f32)
    up_pre = jnp.einsum("esd,edf->esf", inputs, w_up, preferred_element_type=f32)
    grads = in_ring_order(by_expert(routed), along_x, XN)
    grads, gate_pre, up_pre = lax.optimization_barrier((grads, gate_pre, up_pre))
    grads = jnp.concatenate(grads, axis=2)
    grads_far = across_core(grads)

    act_grad = jnp.einsum(
        "esd,efd->esf", grads, down_turned[:, :, :side], preferred_element_type=f32
    ) + jnp.einsum(
        "esd,efd->esf", grads_far, down_turned[:, :, side:], preferred_element_type=f32
    )
    sigmoid_gate = jax.nn.sigmoid(gate_pre)
    gate_grad = (
        act_grad * up_pre * sigmoid_gate * (1.0 + gate_pre * (1.0 - sigmoid_gate))
    ).astype(bf16)
    up_grad = (act_grad * gate_pre * sigmoid_gate).astype(bf16)
    pair_grad = jnp.concatenate([gate_grad, up_grad], axis=2)

    far = jnp.einsum("esf,edf->esd", pair_grad, pair_turned[:, side:], preferred_element_type=f32)
    far = across_core(far.astype(bf16))
    near = jnp.einsum("esf,edf->esd", pair_grad, pair_turned[:, :side], preferred_element_type=f32)
    near = near + far.astype(f32)
    near = near[:, :, :share] + sum(
        along_x(near[:, :, k * share:(k + 1) * share].astype(bf16), k).astype(f32)
        for k in range(1, XN)
    )
    near = near.reshape(own_experts, n_expert, capacity, share)
    near = near.transpose(1, 0, 2, 3).reshape(n_expert, own_experts * capacity, share)
    returned = lax.all_to_all(near, ("y", "z"), 0, 0, tiled=True)
    input_grad = wide_dot(
        pick,
        returned.reshape(experts * capacity, share),
        ((0,), (0,)),
        lax.Precision.HIGHEST,
    )
    return (head_grad, residual_grad, input_grad)


def solution(mesh):
    fine = Mesh(mesh.devices.reshape(YN, ZN, XN, CN), ("y", "z", "x", "core"))
    expert, vocab = ("y", "z"), ("x", "core")
    everywhere = expert + vocab
    in_specs = (
        P(expert, None),
        P(expert, None),
        P(),
        P(None, everywhere),
        P(expert),
        P(expert),
        P(),
        P(expert, None),
        P(expert, None),
        P(expert, None, vocab),
        P(expert, None, vocab),
        P(expert, vocab, None),
    )
    out_specs = (P(None, everywhere), P(expert, vocab), P(expert, vocab))
    return jax.shard_map(
        on_device, mesh=fine, in_specs=in_specs, out_specs=out_specs, check_vma=False
    )
```

```python
import math

import jax
import jax.numpy as jnp
from jax import lax
from jax.experimental import pallas as pl
from jax.experimental.pallas import tpu as pltpu
from jax.sharding import Mesh, PartitionSpec as P

epsilon = 1e-05
YN, ZN, XN, CN = 4, 8, 4, 2
bf16 = jnp.bfloat16
f32 = jnp.float32


def wide_dot(a, b, dims, precision=None):
    return lax.dot_general(
        a, b, (dims, ((), ())), preferred_element_type=f32, precision=precision
    )


def along_y(a, step):
    return lax.ppermute(a, "y", [(p, (p + step) % YN) for p in range(YN)])


def along_x(a, step):
    return lax.ppermute(a, "x", [(p, (p + step) % XN) for p in range(XN)])


def across_core(a):
    return lax.ppermute(a, "core", [(p, CN - 1 - p) for p in range(CN)])


def exchanged(a, axes):
    return lax.all_to_all(a, axes, 0, 0, tiled=True)


def in_ring_order(a, move, ring):
    return [a] + [move(a, ring - k) for k in range(1, ring)]


def normed_to_spread(
    at, layer_out, final_gain, clean_ids, levels, level_count, copies, share
):
    rows, width = layer_out.shape
    below = 8

    def body(
        at_ref, rows_ref, gain_ref, clean_ref, level_ref, spread_out, unit_out, scale_out, gain_out
    ):
        code = jnp.broadcast_to(clean_ref[...] * level_count + level_ref[...], (below, rows))
        line = lax.broadcasted_iota(jnp.int32, (below, rows), 0)
        digits = jnp.where(line == 0, code, jnp.where(line == 1, code >> 8, code >> 16)) & 255
        digits = digits.astype(f32).astype(bf16)
        low = pl.multiple_of(at_ref[0] * share, share)
        values = rows_ref[...].astype(f32)
        mean = jnp.sum(values * values, axis=1, keepdims=True) / width
        scale = jnp.sqrt(mean + epsilon)
        unit = rows_ref[:, pl.ds(low, share)].astype(f32) / scale
        gain = gain_ref[:, pl.ds(low, share)]
        normed = (unit * gain).astype(bf16)
        for k in range(copies):
            spread_out[k, :rows, :] = normed
            spread_out[k, rows:, :] = jnp.zeros((below, share), bf16)
            spread_out[k, rows:, :rows] = digits
        unit_out[...] = unit
        scale_out[...] = scale
        gain_out[...] = gain

    whole = pl.BlockSpec(memory_space=pltpu.VMEM)
    return pl.pallas_call(
        body,
        in_specs=[pl.BlockSpec(memory_space=pltpu.SMEM)] + [whole] * 4,
        out_specs=[whole] * 4,
        out_shape=[
            jax.ShapeDtypeStruct((copies, rows + below, share), bf16),
            jax.ShapeDtypeStruct((rows, share), f32),
            jax.ShapeDtypeStruct((rows, 1), f32),
            jax.ShapeDtypeStruct((1, share), f32),
        ],
        name="normed_to_spread",
    )(at[None], layer_out, final_gain[None, :], clean_ids[None, :], levels[None, :])


def turned_weights(order, head_weight, w_gate, w_up, w_down):
    width, tile = head_weight.shape
    own, _, hidden = w_gate.shape
    count = order.shape[0]
    share = width // count

    lead = count // 2

    def body(
        order_ref, head_ref, gate_ref, up_ref, down_ref, near_out, far_out, pair_out, down_out
    ):
        @pl.when(pl.program_id(0) < lead)
        def _():
            near_out[...] = head_ref[...]

        @pl.when(pl.program_id(0) >= lead)
        def _():
            far_out[...] = head_ref[...]

        pair_out[:, :, :hidden] = gate_ref[...]
        pair_out[:, :, hidden:] = up_ref[...]
        down_out[...] = down_ref[...]

    moved = 2 * (head_weight.size + 3 * w_gate.size)
    return pl.pallas_call(
        body,
        grid_spec=pltpu.PrefetchScalarGridSpec(
            num_scalar_prefetch=1,
            grid=(count,),
            in_specs=[
                pl.BlockSpec((share, tile), lambda i, s: (s[i], 0)),
                pl.BlockSpec((own, share, hidden), lambda i, s: (0, s[i], 0)),
                pl.BlockSpec((own, share, hidden), lambda i, s: (0, s[i], 0)),
                pl.BlockSpec((own, hidden, share), lambda i, s: (0, 0, s[i])),
            ],
            out_specs=[
                pl.BlockSpec((share, tile), lambda i, s: (jnp.minimum(i, lead - 1), 0)),
                pl.BlockSpec((share, tile), lambda i, s: (jnp.maximum(i - lead, 0), 0)),
                pl.BlockSpec((own, share, 2 * hidden), lambda i, s: (0, i, 0)),
                pl.BlockSpec((own, hidden, share), lambda i, s: (0, 0, i)),
            ],
        ),
        out_shape=[
            jax.ShapeDtypeStruct((width // 2, tile), bf16),
            jax.ShapeDtypeStruct((width // 2, tile), bf16),
            jax.ShapeDtypeStruct((own, width, 2 * hidden), bf16),
            jax.ShapeDtypeStruct((own, hidden, width), bf16),
        ],
        cost_estimate=pl.CostEstimate(flops=0, bytes_accessed=2 * moved, transcendentals=0),
        name="turned_weights",
    )(order, head_weight, w_gate, w_up, w_down)


def head_gradient(order, near, far, score_grad):
    rows, side = near.shape
    tile = score_grad.shape[1]
    count = order.shape[0]
    share = 2 * side // count
    lead = count // 2

    def body(order_ref, near_ref, far_ref, grad_ref, out_ref):
        def product(rows_ref):
            out_ref[...] = wide_dot(rows_ref[...], grad_ref[...], ((0,), (0,)))

        @pl.when(pl.program_id(0) < lead)
        def _():
            product(near_ref)

        @pl.when(pl.program_id(0) >= lead)
        def _():
            product(far_ref)

    return pl.pallas_call(
        body,
        grid_spec=pltpu.PrefetchScalarGridSpec(
            num_scalar_prefetch=1,
            grid=(count,),
            in_specs=[
                pl.BlockSpec((rows, share), lambda i, s: (0, jnp.minimum(i, lead - 1))),
                pl.BlockSpec((rows, share), lambda i, s: (0, jnp.maximum(i - lead, 0))),
                pl.BlockSpec((rows, tile), lambda i, s: (0, 0)),
            ],
            out_specs=pl.BlockSpec((share, tile), lambda i, s: (s[i], 0)),
        ),
        out_shape=jax.ShapeDtypeStruct((2 * side, tile), f32),
        cost_estimate=pl.CostEstimate(flops=1024, bytes_accessed=1024, transcendentals=0),
        name="head_gradient",
    )(order, near, far, score_grad)


def near_gradient(score_grad, weight, far):
    rows, tile = score_grad.shape
    share = weight.shape[0] // XN
    part = rows // YN

    def body(grad_ref, weight_ref, far_ref, *outs):
        for k in range(XN):
            low = slice(k * share, (k + 1) * share)
            for i in range(YN):
                at = slice(i * part, (i + 1) * part)
                total = wide_dot(grad_ref[at, :], weight_ref[low, :], ((1,), (1,)))
                total = total + far_ref[at, low].astype(f32)
                outs[k][at, :] = total.astype(outs[k].dtype)

    whole = pl.BlockSpec(memory_space=pltpu.VMEM)
    return pl.pallas_call(
        body,
        in_specs=[whole] * 3,
        out_specs=[whole] * XN,
        out_shape=[
            jax.ShapeDtypeStruct((rows, share), t) for t in [f32] + [bf16] * (XN - 1)
        ],
        cost_estimate=pl.CostEstimate(
            flops=2 * rows * tile * share * XN,
            bytes_accessed=8 * rows * share * XN,
            transcendentals=0,
        ),
        compiler_params=pltpu.CompilerParams(vmem_limit_bytes=16 * 1024 * 1024),
        name="near_gradient",
    )(score_grad, weight, far)


def on_device(
    layer_out,
    moe_input,
    final_gain,
    head_weight,
    clean_ids,
    levels,
    ratio_table,
    gate_weights,
    expert_ids,
    w_gate,
    w_up,
    w_down,
):
    rows, width = layer_out.shape
    n_expert = YN * ZN
    n_vocab = XN * CN
    all_rows = rows * n_expert
    own_experts = w_gate.shape[0]
    experts = own_experts * n_expert
    capacity = max(2, 2 * rows * expert_ids.shape[1] // experts)
    share = width // n_vocab
    tile = head_weight.shape[1]
    y_at, x_at, c_at = lax.axis_index("y"), lax.axis_index("x"), lax.axis_index("core")
    e_at = y_at * ZN + lax.axis_index("z")
    v_at = x_at * CN + c_at

    order = jnp.stack(
        [((x_at + k) % XN) * CN + (c_at + c) % CN for c in range(CN) for k in range(XN)]
    )
    head_near, head_far, pair_turned, down_turned = turned_weights(
        order, head_weight, w_gate, w_up, w_down
    )

    spread, unit_share, row_scale, gain_share = normed_to_spread(
        v_at, layer_out, final_gain, clean_ids, levels, ratio_table.shape[0], n_expert, share
    )

    labels = jnp.arange(experts, dtype=jnp.int32)
    hits = expert_ids[:, :, None] == labels
    naming = jnp.sum(hits.astype(f32), axis=1)
    before = (jnp.arange(rows)[:, None] > jnp.arange(rows)[None, :]).astype(f32)
    earlier = wide_dot(before, naming, ((1,), (0,)))
    gates = jnp.sum(jnp.where(hits, gate_weights[:, :, None], 0.0), axis=1)
    slots = jnp.arange(capacity, dtype=f32)
    taken = (earlier.T[:, None, :] == slots[None, :, None]) & (naming.T[:, None, :] > 0)
    slot_gate = jnp.sum(jnp.where(taken, gates.T[:, None, :], 0.0), axis=2)
    pick = taken.astype(f32).reshape(experts * capacity, rows)
    slot_gate = slot_gate.reshape(experts * capacity, 1)

    def by_expert(a):
        a = a.reshape(n_expert, own_experts, capacity, a.shape[-1])
        return a.transpose(1, 0, 2, 3).reshape(own_experts, n_expert * capacity, a.shape[-1])

    moe_share = lax.dynamic_slice_in_dim(moe_input, v_at * share, share, 1)
    inputs = wide_dot(pick.astype(bf16), moe_share, ((1,), (0,))).astype(bf16)
    inputs = inputs.reshape(n_expert, own_experts * capacity, share)

    spread = exchanged(spread, ("y", "z"))
    spread, head_near, head_far, pair_turned, down_turned, inputs, pick, slot_gate = (
        lax.optimization_barrier(
            (spread, head_near, head_far, pair_turned, down_turned, inputs, pick, slot_gate)
        )
    )
    numbers = spread[:, rows:]
    normed_near = in_ring_order(spread[:, :rows].reshape(all_rows, share), along_x, XN)
    inputs = exchanged(inputs, ("y", "z"))
    normed_near, inputs = lax.optimization_barrier((normed_near, inputs))
    normed_near = jnp.concatenate(normed_near, axis=1)
    normed_far = across_core(normed_near)

    side = width // 2
    numbers = numbers[:, :3, :rows].astype(jnp.int32)
    code_all = numbers[:, 0] + 256 * numbers[:, 1] + 65536 * numbers[:, 2]
    code_all = code_all.reshape(all_rows, 1)
    clean_all = code_all // ratio_table.shape[0]
    level_all = code_all % ratio_table.shape[0]
    level_labels = jnp.arange(ratio_table.shape[0], dtype=jnp.int32)
    ratio_rows = jnp.sum(
        jnp.where(level_all == level_labels[None, :], ratio_table[None, :], 0.0),
        axis=1,
        keepdims=True,
    )
    columns = (e_at * n_vocab + v_at) * tile + jnp.arange(tile, dtype=jnp.int32)
    scores = wide_dot(normed_near, head_near, ((1,), (0,)))
    scores, normed_far = lax.optimization_barrier((scores, normed_far))
    scores = scores + wide_dot(normed_far, head_far, ((1,), (0,)))
    target_hit = (clean_all == columns[None, :]).astype(f32)
    loss_scale = 1.0 / math.sqrt(all_rows)
    score_grad = ((jnp.exp(scores) - ratio_rows * target_hit) * loss_scale).astype(bf16)
    along = jnp.sum(score_grad.astype(f32) * scores, axis=1)
    score_grad, along = lax.optimization_barrier((score_grad, along))
    far = wide_dot(score_grad, head_far, ((1,), (1,))).astype(bf16)
    far = across_core(far)
    kept, *sent = near_gradient(score_grad, head_near, far)
    kept, sent, score_grad, along = lax.optimization_barrier((kept, sent, score_grad, along))
    sent = [along_x(a, k + 1) for k, a in enumerate(sent)]
    along = jnp.pad(along.reshape(n_expert, 1, rows), ((0, 0), (0, 7), (0, 128 - rows)))
    along = jnp.sum(exchanged(along, ("y", "z")), axis=0)
    head_grad = head_gradient(order, normed_near, normed_far, score_grad)
    inputs = by_expert(inputs)
    sent, head_grad, along, inputs = lax.optimization_barrier((sent, head_grad, along, inputs))
    inputs = lax.all_gather(inputs, ("x", "core"), axis=2, tiled=True)
    along = along + across_core(along)
    along = along + sum(along_x(along, k) for k in range(1, XN))
    kept = (kept + sum(a.astype(f32) for a in sent)).astype(bf16)
    kept = exchanged(kept.reshape(n_expert, rows, share), ("y", "z"))
    normed_grad = jnp.sum(kept.astype(f32), axis=0)

    residual_grad = (
        gain_share * normed_grad - unit_share * (along[0, :rows] / width)[:, None]
    ) / row_scale

    routed = wide_dot(pick, residual_grad, ((1,), (0,)), lax.Precision.HIGHEST)
    routed = (slot_gate * routed).astype(bf16).reshape(n_expert, own_experts * capacity, share)
    routed = exchanged(routed, ("y", "z"))
    gate_pre = jnp.einsum("esd,edf->esf", inputs, w_gate, preferred_element_type=f32)
    up_pre = jnp.einsum("esd,edf->esf", inputs, w_up, preferred_element_type=f32)
    grads = in_ring_order(by_expert(routed), along_x, XN)
    grads, gate_pre, up_pre = lax.optimization_barrier((grads, gate_pre, up_pre))
    grads = jnp.concatenate(grads, axis=2)
    grads_far = across_core(grads)

    act_grad = jnp.einsum(
        "esd,efd->esf", grads, down_turned[:, :, :side], preferred_element_type=f32
    )
    act_grad, grads_far = lax.optimization_barrier((act_grad, grads_far))
    act_grad = act_grad + jnp.einsum(
        "esd,efd->esf", grads_far, down_turned[:, :, side:], preferred_element_type=f32
    )
    sigmoid_gate = jax.nn.sigmoid(gate_pre)
    gate_grad = (
        act_grad * up_pre * sigmoid_gate * (1.0 + gate_pre * (1.0 - sigmoid_gate))
    ).astype(bf16)
    up_grad = (act_grad * gate_pre * sigmoid_gate).astype(bf16)
    pair_grad = jnp.concatenate([gate_grad, up_grad], axis=2)

    far = jnp.einsum("esf,edf->esd", pair_grad, pair_turned[:, side:], preferred_element_type=f32)
    far = across_core(far.astype(bf16))
    near = jnp.einsum("esf,edf->esd", pair_grad, pair_turned[:, :side], preferred_element_type=f32)
    near, far = lax.optimization_barrier((near, far))
    near = near + far.astype(f32)
    near = near[:, :, :share] + sum(
        along_x(near[:, :, k * share:(k + 1) * share].astype(bf16), k).astype(f32)
        for k in range(1, XN)
    )
    near = near.reshape(own_experts, n_expert, capacity, share)
    near = near.transpose(1, 0, 2, 3).reshape(n_expert, own_experts * capacity, share)
    returned = lax.all_to_all(near, ("y", "z"), 0, 0, tiled=True)
    input_grad = wide_dot(
        pick,
        returned.reshape(experts * capacity, share),
        ((0,), (0,)),
        lax.Precision.HIGHEST,
    )
    return (head_grad, residual_grad, input_grad)


def solution(mesh):
    fine = Mesh(mesh.devices.reshape(YN, ZN, XN, CN), ("y", "z", "x", "core"))
    expert, vocab = ("y", "z"), ("x", "core")
    everywhere = expert + vocab
    in_specs = (
        P(expert, None),
        P(expert, None),
        P(),
        P(None, everywhere),
        P(expert),
        P(expert),
        P(),
        P(expert, None),
        P(expert, None),
        P(expert, None, vocab),
        P(expert, None, vocab),
        P(expert, vocab, None),
    )
    out_specs = (P(None, everywhere), P(expert, vocab), P(expert, vocab))
    return jax.shard_map(
        on_device, mesh=fine, in_specs=in_specs, out_specs=out_specs, check_vma=False
    )
```

```python
import math

import jax
import jax.numpy as jnp
from jax import lax
from jax.experimental import pallas as pl
from jax.experimental.pallas import tpu as pltpu
from jax.sharding import Mesh, PartitionSpec as P

epsilon = 1e-05
YN, ZN, XN, CN = 4, 8, 4, 2
bf16 = jnp.bfloat16
f32 = jnp.float32


def wide_dot(a, b, dims, precision=None):
    return lax.dot_general(
        a, b, (dims, ((), ())), preferred_element_type=f32, precision=precision
    )


def along_y(a, step):
    return lax.ppermute(a, "y", [(p, (p + step) % YN) for p in range(YN)])


def along_x(a, step):
    return lax.ppermute(a, "x", [(p, (p + step) % XN) for p in range(XN)])


def across_core(a):
    return lax.ppermute(a, "core", [(p, CN - 1 - p) for p in range(CN)])


def exchanged(a, axes):
    return lax.all_to_all(a, axes, 0, 0, tiled=True)


def in_ring_order(a, move, ring):
    near = sorted(range(1, ring), key=lambda k: min(k, ring - k))
    moved = {k: move(a, ring - k) for k in near}
    return [a] + [moved[k] for k in range(1, ring)]


def normed_to_spread(
    at, layer_out, final_gain, clean_ids, levels, level_count, copies, share
):
    rows, width = layer_out.shape
    below = 8

    def body(
        at_ref, rows_ref, gain_ref, clean_ref, level_ref, spread_out, unit_out, scale_out, gain_out
    ):
        code = jnp.broadcast_to(clean_ref[...] * level_count + level_ref[...], (below, rows))
        line = lax.broadcasted_iota(jnp.int32, (below, rows), 0)
        digits = jnp.where(line == 0, code, jnp.where(line == 1, code >> 8, code >> 16)) & 255
        digits = digits.astype(f32).astype(bf16)
        low = pl.multiple_of(at_ref[0] * share, share)
        values = rows_ref[...].astype(f32)
        mean = jnp.sum(values * values, axis=1, keepdims=True) / width
        scale = jnp.sqrt(mean + epsilon)
        unit = rows_ref[:, pl.ds(low, share)].astype(f32) / scale
        gain = gain_ref[:, pl.ds(low, share)]
        normed = (unit * gain).astype(bf16)
        for k in range(copies):
            spread_out[k, :rows, :] = normed
            spread_out[k, rows:, :] = jnp.zeros((below, share), bf16)
            spread_out[k, rows:, :rows] = digits
        unit_out[...] = unit
        scale_out[...] = scale
        gain_out[...] = gain

    whole = pl.BlockSpec(memory_space=pltpu.VMEM)
    return pl.pallas_call(
        body,
        in_specs=[pl.BlockSpec(memory_space=pltpu.SMEM)] + [whole] * 4,
        out_specs=[whole] * 4,
        out_shape=[
            jax.ShapeDtypeStruct((copies, rows + below, share), bf16),
            jax.ShapeDtypeStruct((rows, share), f32),
            jax.ShapeDtypeStruct((rows, 1), f32),
            jax.ShapeDtypeStruct((1, share), f32),
        ],
        name="normed_to_spread",
    )(at[None], layer_out, final_gain[None, :], clean_ids[None, :], levels[None, :])


def turned_weights(order, head_weight, w_gate, w_up, w_down):
    width, tile = head_weight.shape
    own, _, hidden = w_gate.shape
    count = order.shape[0]
    share = width // count

    lead = count // 2

    def body(
        order_ref, head_ref, gate_ref, up_ref, down_ref, near_out, far_out, pair_out, down_out
    ):
        @pl.when(pl.program_id(0) < lead)
        def _():
            near_out[...] = head_ref[...]

        @pl.when(pl.program_id(0) >= lead)
        def _():
            far_out[...] = head_ref[...]

        pair_out[:, :, :hidden] = gate_ref[...]
        pair_out[:, :, hidden:] = up_ref[...]
        down_out[...] = down_ref[...]

    moved = 2 * (head_weight.size + 3 * w_gate.size)
    return pl.pallas_call(
        body,
        grid_spec=pltpu.PrefetchScalarGridSpec(
            num_scalar_prefetch=1,
            grid=(count,),
            in_specs=[
                pl.BlockSpec((share, tile), lambda i, s: (s[i], 0)),
                pl.BlockSpec((own, share, hidden), lambda i, s: (0, s[i], 0)),
                pl.BlockSpec((own, share, hidden), lambda i, s: (0, s[i], 0)),
                pl.BlockSpec((own, hidden, share), lambda i, s: (0, 0, s[i])),
            ],
            out_specs=[
                pl.BlockSpec((share, tile), lambda i, s: (jnp.minimum(i, lead - 1), 0)),
                pl.BlockSpec((share, tile), lambda i, s: (jnp.maximum(i - lead, 0), 0)),
                pl.BlockSpec((own, share, 2 * hidden), lambda i, s: (0, i, 0)),
                pl.BlockSpec((own, hidden, share), lambda i, s: (0, 0, i)),
            ],
        ),
        out_shape=[
            jax.ShapeDtypeStruct((width // 2, tile), bf16),
            jax.ShapeDtypeStruct((width // 2, tile), bf16),
            jax.ShapeDtypeStruct((own, width, 2 * hidden), bf16),
            jax.ShapeDtypeStruct((own, hidden, width), bf16),
        ],
        cost_estimate=pl.CostEstimate(flops=0, bytes_accessed=2 * moved, transcendentals=0),
        name="turned_weights",
    )(order, head_weight, w_gate, w_up, w_down)


def head_gradient(order, near, far, score_grad):
    rows, side = near.shape
    tile = score_grad.shape[1]
    count = order.shape[0]
    share = 2 * side // count
    lead = count // 2

    def body(order_ref, near_ref, far_ref, grad_ref, out_ref):
        def product(rows_ref):
            out_ref[...] = wide_dot(rows_ref[...], grad_ref[...], ((0,), (0,)))

        @pl.when(pl.program_id(0) < lead)
        def _():
            product(near_ref)

        @pl.when(pl.program_id(0) >= lead)
        def _():
            product(far_ref)

    return pl.pallas_call(
        body,
        grid_spec=pltpu.PrefetchScalarGridSpec(
            num_scalar_prefetch=1,
            grid=(count,),
            in_specs=[
                pl.BlockSpec((rows, share), lambda i, s: (0, jnp.minimum(i, lead - 1))),
                pl.BlockSpec((rows, share), lambda i, s: (0, jnp.maximum(i - lead, 0))),
                pl.BlockSpec((rows, tile), lambda i, s: (0, 0)),
            ],
            out_specs=pl.BlockSpec((share, tile), lambda i, s: (s[i], 0)),
        ),
        out_shape=jax.ShapeDtypeStruct((2 * side, tile), f32),
        cost_estimate=pl.CostEstimate(flops=1024, bytes_accessed=1024, transcendentals=0),
        name="head_gradient",
    )(order, near, far, score_grad)


def near_gradient(score_grad, weight, far):
    rows, tile = score_grad.shape
    share = weight.shape[0] // XN
    part = rows // YN

    def body(grad_ref, weight_ref, far_ref, *outs):
        for k in range(XN):
            low = slice(k * share, (k + 1) * share)
            for i in range(YN):
                at = slice(i * part, (i + 1) * part)
                total = wide_dot(grad_ref[at, :], weight_ref[low, :], ((1,), (1,)))
                total = total + far_ref[at, low].astype(f32)
                outs[k][at, :] = total.astype(outs[k].dtype)

    whole = pl.BlockSpec(memory_space=pltpu.VMEM)
    return pl.pallas_call(
        body,
        in_specs=[whole] * 3,
        out_specs=[whole] * XN,
        out_shape=[
            jax.ShapeDtypeStruct((rows, share), t) for t in [f32] + [bf16] * (XN - 1)
        ],
        cost_estimate=pl.CostEstimate(
            flops=2 * rows * tile * share * XN,
            bytes_accessed=8 * rows * share * XN,
            transcendentals=0,
        ),
        compiler_params=pltpu.CompilerParams(vmem_limit_bytes=16 * 1024 * 1024),
        name="near_gradient",
    )(score_grad, weight, far)


def on_device(
    layer_out,
    moe_input,
    final_gain,
    head_weight,
    clean_ids,
    levels,
    ratio_table,
    gate_weights,
    expert_ids,
    w_gate,
    w_up,
    w_down,
):
    rows, width = layer_out.shape
    n_expert = YN * ZN
    n_vocab = XN * CN
    all_rows = rows * n_expert
    own_experts = w_gate.shape[0]
    experts = own_experts * n_expert
    capacity = max(2, 2 * rows * expert_ids.shape[1] // experts)
    share = width // n_vocab
    tile = head_weight.shape[1]
    y_at, x_at, c_at = lax.axis_index("y"), lax.axis_index("x"), lax.axis_index("core")
    e_at = y_at * ZN + lax.axis_index("z")
    v_at = x_at * CN + c_at

    order = jnp.stack(
        [((x_at + k) % XN) * CN + (c_at + c) % CN for c in range(CN) for k in range(XN)]
    )
    head_near, head_far, pair_turned, down_turned = turned_weights(
        order, head_weight, w_gate, w_up, w_down
    )

    spread, unit_share, row_scale, gain_share = normed_to_spread(
        v_at, layer_out, final_gain, clean_ids, levels, ratio_table.shape[0], n_expert, share
    )

    labels = jnp.arange(experts, dtype=jnp.int32)
    hits = expert_ids[:, :, None] == labels
    naming = jnp.sum(hits.astype(f32), axis=1)
    before = (jnp.arange(rows)[:, None] > jnp.arange(rows)[None, :]).astype(f32)
    earlier = wide_dot(before, naming, ((1,), (0,)))
    gates = jnp.sum(jnp.where(hits, gate_weights[:, :, None], 0.0), axis=1)
    slots = jnp.arange(capacity, dtype=f32)
    taken = (earlier.T[:, None, :] == slots[None, :, None]) & (naming.T[:, None, :] > 0)
    slot_gate = jnp.sum(jnp.where(taken, gates.T[:, None, :], 0.0), axis=2)
    pick = taken.astype(f32).reshape(experts * capacity, rows)
    slot_gate = slot_gate.reshape(experts * capacity, 1)

    def by_expert(a):
        a = a.reshape(n_expert, own_experts, capacity, a.shape[-1])
        return a.transpose(1, 0, 2, 3).reshape(own_experts, n_expert * capacity, a.shape[-1])

    moe_share = lax.dynamic_slice_in_dim(moe_input, v_at * share, share, 1)
    inputs = wide_dot(pick.astype(bf16), moe_share, ((1,), (0,))).astype(bf16)
    inputs = inputs.reshape(n_expert, own_experts * capacity, share)

    spread = exchanged(spread, ("y", "z"))
    spread, head_near, head_far, pair_turned, down_turned, inputs, pick, slot_gate = (
        lax.optimization_barrier(
            (spread, head_near, head_far, pair_turned, down_turned, inputs, pick, slot_gate)
        )
    )
    numbers = spread[:, rows:]
    normed_near = in_ring_order(spread[:, :rows].reshape(all_rows, share), along_x, XN)
    inputs = exchanged(inputs, ("y", "z"))
    normed_near, inputs = lax.optimization_barrier((normed_near, inputs))
    normed_near = jnp.concatenate(normed_near, axis=1)
    normed_far = across_core(normed_near)

    side = width // 2
    numbers = numbers[:, :3, :rows].astype(jnp.int32)
    code_all = numbers[:, 0] + 256 * numbers[:, 1] + 65536 * numbers[:, 2]
    code_all = code_all.reshape(all_rows, 1)
    clean_all = code_all // ratio_table.shape[0]
    level_all = code_all % ratio_table.shape[0]
    level_labels = jnp.arange(ratio_table.shape[0], dtype=jnp.int32)
    ratio_rows = jnp.sum(
        jnp.where(level_all == level_labels[None, :], ratio_table[None, :], 0.0),
        axis=1,
        keepdims=True,
    )
    columns = (e_at * n_vocab + v_at) * tile + jnp.arange(tile, dtype=jnp.int32)
    scores = wide_dot(normed_near, head_near, ((1,), (0,)))
    scores, normed_far = lax.optimization_barrier((scores, normed_far))
    scores = scores + wide_dot(normed_far, head_far, ((1,), (0,)))
    target_hit = (clean_all == columns[None, :]).astype(f32)
    loss_scale = 1.0 / math.sqrt(all_rows)
    score_grad = ((jnp.exp(scores) - ratio_rows * target_hit) * loss_scale).astype(bf16)
    along = jnp.sum(score_grad.astype(f32) * scores, axis=1)
    score_grad, along = lax.optimization_barrier((score_grad, along))
    far = wide_dot(score_grad, head_far, ((1,), (1,))).astype(bf16)
    far = across_core(far)
    kept, *sent = near_gradient(score_grad, head_near, far)
    kept, sent, score_grad, along = lax.optimization_barrier((kept, sent, score_grad, along))
    sent = [along_x(sent[k - 1], k) for k in (2, 1, 3)]
    along = jnp.pad(along.reshape(n_expert, 1, rows), ((0, 0), (0, 7), (0, 128 - rows)))
    along = jnp.sum(exchanged(along, ("y", "z")), axis=0)
    head_grad = head_gradient(order, normed_near, normed_far, score_grad)
    inputs = by_expert(inputs)
    sent, head_grad, along, inputs = lax.optimization_barrier((sent, head_grad, along, inputs))
    inputs = lax.all_gather(inputs, ("x", "core"), axis=2, tiled=True)
    along = along + across_core(along)
    along = along + sum(along_x(along, k) for k in range(1, XN))
    kept = (kept + sum(a.astype(f32) for a in sent)).astype(bf16)
    kept = exchanged(kept.reshape(n_expert, rows, share), ("y", "z"))
    normed_grad = jnp.sum(kept.astype(f32), axis=0)

    residual_grad = (
        gain_share * normed_grad - unit_share * (along[0, :rows] / width)[:, None]
    ) / row_scale

    routed = wide_dot(pick, residual_grad, ((1,), (0,)), lax.Precision.HIGHEST)
    routed = (slot_gate * routed).astype(bf16).reshape(n_expert, own_experts * capacity, share)
    routed = exchanged(routed, ("y", "z"))
    gate_pre = jnp.einsum("esd,edf->esf", inputs, w_gate, preferred_element_type=f32)
    up_pre = jnp.einsum("esd,edf->esf", inputs, w_up, preferred_element_type=f32)
    grads = in_ring_order(by_expert(routed), along_x, XN)
    grads, gate_pre, up_pre = lax.optimization_barrier((grads, gate_pre, up_pre))
    grads = jnp.concatenate(grads, axis=2)
    grads_far = across_core(grads)

    act_grad = jnp.einsum(
        "esd,efd->esf", grads, down_turned[:, :, :side], preferred_element_type=f32
    )
    act_grad, grads_far = lax.optimization_barrier((act_grad, grads_far))
    act_grad = act_grad + jnp.einsum(
        "esd,efd->esf", grads_far, down_turned[:, :, side:], preferred_element_type=f32
    )
    sigmoid_gate = jax.nn.sigmoid(gate_pre)
    gate_grad = (
        act_grad * up_pre * sigmoid_gate * (1.0 + gate_pre * (1.0 - sigmoid_gate))
    ).astype(bf16)
    up_grad = (act_grad * gate_pre * sigmoid_gate).astype(bf16)
    pair_grad = jnp.concatenate([gate_grad, up_grad], axis=2)

    far = jnp.einsum("esf,edf->esd", pair_grad, pair_turned[:, side:], preferred_element_type=f32)
    far = across_core(far.astype(bf16))
    near = jnp.einsum("esf,edf->esd", pair_grad, pair_turned[:, :side], preferred_element_type=f32)
    near, far = lax.optimization_barrier((near, far))
    near = near + far.astype(f32)
    near = near[:, :, :share] + sum(
        along_x(near[:, :, k * share:(k + 1) * share].astype(bf16), k).astype(f32)
        for k in range(1, XN)
    )
    near = near.reshape(own_experts, n_expert, capacity, share)
    near = near.transpose(1, 0, 2, 3).reshape(n_expert, own_experts * capacity, share)
    returned = lax.all_to_all(near, ("y", "z"), 0, 0, tiled=True)
    input_grad = wide_dot(
        pick,
        returned.reshape(experts * capacity, share),
        ((0,), (0,)),
        lax.Precision.HIGHEST,
    )
    return (head_grad, residual_grad, input_grad)


def solution(mesh):
    fine = Mesh(mesh.devices.reshape(YN, ZN, XN, CN), ("y", "z", "x", "core"))
    expert, vocab = ("y", "z"), ("x", "core")
    everywhere = expert + vocab
    in_specs = (
        P(expert, None),
        P(expert, None),
        P(),
        P(None, everywhere),
        P(expert),
        P(expert),
        P(),
        P(expert, None),
        P(expert, None),
        P(expert, None, vocab),
        P(expert, None, vocab),
        P(expert, vocab, None),
    )
    out_specs = (P(None, everywhere), P(expert, vocab), P(expert, vocab))
    return jax.shard_map(
        on_device, mesh=fine, in_specs=in_specs, out_specs=out_specs, check_vma=False
    )
```
